512 devices in a mesh: tile: 32 (over z_lo, x, core), head: 16 (over z_hi, y).
Axes of the slice: x: 4, y: 4, z: 16 (z_hi: 4, z_lo: 4; z = z_hi * 4 + z_lo), core: 2. Of those that a mesh axis runs over, the one named last changes fastest.
Arguments:
- tokens: bfloat16 [8192, 1024], P('tile'), may hold values from -40 to 40
- w_qkv: bfloat16 [3072, 1024], P('head'), may hold values from -0.125 to 0.125
- grad_out: bfloat16 [8192, 1024], P('tile', 'head'), may hold values from -6 to 6
- edge_valid: int32 [32, 8], P('tile'), may hold values 0 or 1
Outputs:
- grad_x: bfloat16 [8192, 1024], P(('tile', 'head'))
- grad_w: float32 [1024, 3072], P('tile', 'head')
The draws below stay inside these ranges and needn't reach their ends.
All inputs are finite; a program needn't handle non-finite values. No bound on the sum of `edge_valid` on one device may be relied on, other than what follows from the above.
Results may differ from the reference program's by a relative error of at most 0.024.
Values may be sent and summed in bfloat16 or wider, within the bound.
No kernel may reach another device: no remote copies, remote signals or barrier semaphores. Data moves between devices by JAX's collectives and lax.ppermute only.
A program may use at most 64 MiB of HBM per device.

```python
import jax
import jax.numpy as jnp
from jax import lax

D = 1024
HEADS = 16
HEAD_DIM = 64
HALO = 12
S = 16
GRID_ROWS = 4
GRID_COLS = 8
TILES = 32
TOKENS = 8192
N_HEAD = 16


def draw_tokens(key, part):
    base_key = jax.random.fold_in(jax.random.fold_in(key, 11), 0)
    base = jax.random.truncated_normal(base_key, -6.0, 6.0, (TOKENS, D), jnp.float32)
    return base.astype(jnp.bfloat16)


def draw_w_qkv(key, part):
    head_width = D // HEADS
    raw = jax.random.normal(jax.random.fold_in(key, 23), (D, HEADS, 3, head_width), jnp.float32) * D ** (-0.5)
    raw = jnp.clip(raw, -0.125, 0.125)
    return jnp.transpose(raw.reshape(D, HEADS * 3 * head_width)).astype(jnp.bfloat16)


def with_ends(array, stream_key, smallest, top_value):
    dims = array.shape
    index_at = [jax.random.randint(jax.random.fold_in(stream_key, axis), (), 0, dims[axis]) for axis in range(len(dims))]
    array = array.at[tuple(index_at)].set(smallest)
    longest = dims.index(max(dims))
    index_at[longest] = (index_at[longest] + 1) % dims[longest]
    return array.at[tuple(index_at)].set(top_value)


def steps_of(own_key, dims, pieces, low, high):
    level, own = 1.0, jax.random.fold_in(own_key, 6)
    for dim, parts in pieces:
        steps = jnp.exp(jax.random.uniform(jax.random.fold_in(own, dim), (parts,), jnp.float32, low / len(pieces), high / len(pieces)))
        level = level * jnp.repeat(steps, dims[dim] // parts).reshape([-1 if axis == dim else 1 for axis in range(len(dims))])
    return level


def bell_draw(rng, dims, scale, limit, pieces=(), kind=jnp.bfloat16):
    factor_of = steps_of(rng, dims, pieces, -0.22, 0.18) if pieces else 1.0
    result = jax.random.normal(rng, dims, jnp.float32) * scale * factor_of
    return jnp.minimum(jnp.maximum(result, -limit), limit).astype(kind)


def setup_inputs(seed: int = 0) -> dict:
    seeds = jax.random.split(jax.random.key(seed), 5)
    return {
        "tokens": draw_tokens(jax.random.fold_in(seeds[4], 71), 0),
        "w_qkv": draw_w_qkv(jax.random.fold_in(seeds[4], 71), 0),
        "grad_out": bell_draw(seeds[2], (TOKENS, HEADS * HEAD_DIM), 1.0, 6.0, ((0, 32), (1, 16))),
        "edge_valid": with_ends((jax.random.randint(seeds[3], (TILES, 8), 0, 4) < 3).astype(jnp.int32), jax.random.fold_in(seeds[3], 1), 0, 1),
    }


directions = ((-1, -1), (-1, 0), (-1, 1), (0, -1), (0, 1), (1, -1), (1, 0), (1, 1))


def usable_region(flags, grid_row, grid_col, side, halo):
    width = side + 2 * halo
    place = jnp.arange(width)
    bands = (place >= halo).astype(jnp.int32) + (place >= halo + side).astype(jnp.int32)
    usable = ((bands[:, None] == 1) & (bands[None, :] == 1)).astype(jnp.int32)
    for number, (row_step, column_step) in enumerate(directions):
        inside = (grid_row + row_step >= 0) & (grid_row + row_step < GRID_ROWS)
        inside = inside & (grid_col + column_step >= 0) & (grid_col + column_step < GRID_COLS)
        flag = flags[number] * inside.astype(jnp.int32)
        strike = (bands[:, None] == row_step + 1) & (bands[None, :] == column_step + 1)
        usable = usable + flag * strike.astype(jnp.int32)
    return usable > 0


def window_mask(height, side, halo):
    width = side + 2 * halo
    query_row = jnp.arange(height)[:, None, None, None]
    query_column = jnp.arange(side)[None, :, None, None]
    key_row = jnp.arange(height + 2 * halo)[None, None, :, None]
    key_column = jnp.arange(width)[None, None, None, :]
    near = (jnp.abs(key_row - query_row - halo) <= halo) & (jnp.abs(key_column - query_column - halo) <= halo)
    return near.reshape(height * side, (height + 2 * halo) * width)


def band_backward(query, keys, values, grads, allowed):
    scale = query.shape[-1] ** -0.5
    query = query.astype(jnp.float32)
    keys = keys.astype(jnp.float32)
    values = values.astype(jnp.float32)
    grads = grads.astype(jnp.float32)
    scores = jnp.einsum("qhe,khe->hqk", query, keys) * scale
    scores = jnp.where(allowed[None], scores, -1e30)
    highest = jnp.max(scores, axis=2, keepdims=True)
    lifted = jnp.exp(scores - highest)
    probs = lifted / jnp.sum(lifted, axis=2, keepdims=True)
    probs_low = probs.astype(jnp.bfloat16).astype(jnp.float32)
    attended = jnp.einsum("hqk,khe->qhe", probs_low, values)
    row_dot = jnp.sum(grads * attended, axis=2)
    grad_probs = jnp.einsum("qhe,khe->hqk", grads, values)
    grad_scores = (probs * (grad_probs - jnp.transpose(row_dot)[:, :, None])).astype(jnp.bfloat16).astype(jnp.float32)
    grad_query = jnp.einsum("hqk,khe->qhe", grad_scores, keys) * scale
    grad_keys = jnp.einsum("hqk,qhe->khe", grad_scores, query) * scale
    grad_values = jnp.einsum("hqk,qhe->khe", probs_low, grads)
    return grad_query, grad_keys, grad_values


def reference(tokens, w_qkv, grad_out, edge_valid):
    side = S
    halo = HALO
    width = side + 2 * halo
    head_width = D // HEADS
    columns = GRID_COLS
    weights = jnp.transpose(w_qkv)
    projected = jnp.dot(tokens, weights, preferred_element_type=jnp.float32).astype(jnp.bfloat16)
    per_tile = projected.reshape(TILES, side, side, HEADS, 3, head_width)
    queries = per_tile[:, :, :, :, 0].reshape(TILES, side * side, HEADS, head_width)
    grid = per_tile[:, :, :, :, 1:].reshape(GRID_ROWS, columns, side, side, HEADS, 2, head_width)
    grid = jnp.transpose(grid, (0, 2, 1, 3, 4, 5, 6)).reshape(GRID_ROWS * side, columns * side, HEADS, 2, head_width)
    padded = jnp.pad(grid, ((halo, halo), (halo, halo), (0, 0), (0, 0), (0, 0)))
    grads = grad_out.reshape(TILES, side * side, HEADS, head_width)
    near = window_mask(side, side, halo)
    zero = jnp.zeros((), jnp.int32)

    def one_tile(carry, inputs):
        number, query, grad_tile, flags = inputs
        grid_row = number // columns
        grid_col = number % columns
        usable = usable_region(flags, grid_row, grid_col, side, halo)
        start = ((grid_row * side).astype(jnp.int32), (grid_col * side).astype(jnp.int32), zero, zero, zero)
        region = lax.dynamic_slice(padded, start, (width, width, HEADS, 2, head_width))
        keys = region[:, :, :, 0].reshape(width * width, HEADS, head_width)
        values = region[:, :, :, 1].reshape(width * width, HEADS, head_width)
        allowed = near & usable.reshape(1, -1)
        grad_query, grad_keys, grad_values = band_backward(query, keys, values, grad_tile, allowed)
        both = jnp.stack([grad_keys, grad_values], axis=2).reshape(width, width, HEADS, 2, head_width)
        current = lax.dynamic_slice(carry, start, (width, width, HEADS, 2, head_width))
        carry = lax.dynamic_update_slice(carry, current + both, start)
        return carry, grad_query

    numbers = jnp.arange(TILES, dtype=jnp.int32)
    carry, grad_queries = lax.scan(one_tile, jnp.zeros(padded.shape, jnp.float32), (numbers, queries, grads, edge_valid))
    inner = carry[halo:halo + GRID_ROWS * side, halo:halo + columns * side]
    inner = inner.reshape(GRID_ROWS, side, columns, side, HEADS, 2, head_width)
    inner = jnp.transpose(inner, (0, 2, 1, 3, 4, 5, 6)).reshape(TOKENS, HEADS, 2, head_width)
    grad_queries = grad_queries.reshape(TOKENS, HEADS, 1, head_width)
    grad_qkv = jnp.concatenate([grad_queries, inner], axis=2).reshape(TOKENS, HEADS * 3 * head_width).astype(jnp.bfloat16)
    grad_w = jnp.dot(jnp.transpose(tokens), grad_qkv, preferred_element_type=jnp.float32)
    group_grads = jnp.transpose(grad_qkv.reshape(TOKENS, N_HEAD, -1), (1, 0, 2))
    group_weights = jnp.transpose(weights.reshape(D, N_HEAD, -1), (1, 0, 2))

    def add_group(total, pair):
        left, right = pair
        partial_value = lax.dot_general(left, right, (((1,), (1,)), ((), ())), preferred_element_type=jnp.float32).astype(jnp.bfloat16)
        partial_value = lax.optimization_barrier(partial_value)
        return total + partial_value.astype(jnp.float32), None

    total, unused = lax.scan(add_group, jnp.zeros((TOKENS, D), jnp.float32), (group_grads, group_weights))
    return total.astype(jnp.bfloat16), grad_w
```

```python
import jax
import jax.numpy as jnp
from jax import lax
from jax.sharding import PartitionSpec as P

D = 1024
HEADS = 16
HALO = 12
S = 16
GRID_ROWS = 4


directions = ((-1, -1), (-1, 0), (-1, 1), (0, -1), (0, 1), (1, -1), (1, 0), (1, 1))
band_height = 16
NEAR = 4
HIGH = 4
near_groups = [[high * NEAR + near for near in range(NEAR)] for high in range(HIGH)]
far_groups = [[high * NEAR + near for high in range(HIGH)] for near in range(NEAR)]


def summed_exchange(chunks, axis, groups):
    received = lax.all_to_all(chunks, axis, 0, 0, axis_index_groups=groups)
    return jnp.sum(received.astype(jnp.float32), axis=0)


def passed_along(value, axis, steps):
    count = lax.axis_size(axis)
    first, last = (max(0, -steps), min(count, count - steps))
    return lax.ppermute(value, axis, [(source, source + steps) for source in range(first, last)])


def source_span(offset, side, halo):
    if offset == -1:
        return (side - halo, side)
    if offset == 1:
        return (0, halo)
    return (0, side)


def target_span(offset, side, halo):
    if offset == -1:
        return (0, halo)
    if offset == 1:
        return (halo + side, side + 2 * halo)
    return (halo, halo + side)


def usable_region(flags, grid_row, grid_col, columns, side, halo):
    width = side + 2 * halo
    place = jnp.arange(width)
    bands = (place >= halo).astype(jnp.int32) + (place >= halo + side).astype(jnp.int32)
    usable = ((bands[:, None] == 1) & (bands[None, :] == 1)).astype(jnp.int32)
    for number, (row_step, column_step) in enumerate(directions):
        inside = (grid_row + row_step >= 0) & (grid_row + row_step < GRID_ROWS)
        inside = inside & (grid_col + column_step >= 0) & (grid_col + column_step < columns)
        flag = flags[number] * inside.astype(jnp.int32)
        strike = (bands[:, None] == row_step + 1) & (bands[None, :] == column_step + 1)
        usable = usable + flag * strike.astype(jnp.int32)
    return usable > 0


def window_mask(height, side, halo):
    width = side + 2 * halo
    query_row = jnp.arange(height)[:, None, None, None]
    query_column = jnp.arange(side)[None, :, None, None]
    key_row = jnp.arange(height + 2 * halo)[None, None, :, None]
    key_column = jnp.arange(width)[None, None, None, :]
    near = (jnp.abs(key_row - query_row - halo) <= halo) & (
        jnp.abs(key_column - query_column - halo) <= halo
    )
    return near.reshape(height * side, (height + 2 * halo) * width)


def band_backward(query, keys, values, grads, allowed):
    scale = query.shape[-1] ** (-0.5)
    scores = jnp.einsum("qhe,khe->hqk", query, keys, preferred_element_type=jnp.float32) * scale
    scores = jnp.where(allowed[None], scores, -1e30)
    highest = jnp.max(scores, axis=2, keepdims=True)
    lifted = jnp.exp(scores - highest)
    probs = lifted / jnp.sum(lifted, axis=2, keepdims=True)
    probs_low = probs.astype(jnp.bfloat16)
    attended = jnp.einsum("hqk,khe->qhe", probs_low, values, preferred_element_type=jnp.float32)
    row_dot = jnp.sum(grads.astype(jnp.float32) * attended, axis=2)
    grad_probs = jnp.einsum("qhe,khe->hqk", grads, values, preferred_element_type=jnp.float32)
    grad_scores = (probs * (grad_probs - jnp.transpose(row_dot)[:, :, None])).astype(jnp.bfloat16)
    grad_query = (
        jnp.einsum("hqk,khe->qhe", grad_scores, keys, preferred_element_type=jnp.float32) * scale
    )
    grad_keys = (
        jnp.einsum("hqk,qhe->khe", grad_scores, query, preferred_element_type=jnp.float32) * scale
    )
    grad_values = jnp.einsum("hqk,qhe->khe", probs_low, grads, preferred_element_type=jnp.float32)
    return (grad_query, grad_keys, grad_values)


def shards(tokens, w_qkv, grad_out, edge_valid):
    side = S
    halo = HALO
    width = side + 2 * halo
    head_width = D // HEADS
    tiles = lax.axis_size("tile")
    columns = tiles // GRID_ROWS
    number = lax.axis_index("tile")
    grid_row = number // columns
    grid_col = number % columns
    local_heads = w_qkv.shape[0] // (3 * head_width)
    projected = lax.dot_general(
        tokens, w_qkv, (((1,), (1,)), ((), ())), preferred_element_type=jnp.float32
    ).astype(jnp.bfloat16)
    arranged = projected.reshape(side, side, local_heads, 3 * head_width)
    queries = arranged[:, :, :, :head_width]
    pairs = arranged[:, :, :, head_width:]
    region = jnp.zeros((width, width, local_heads, 2 * head_width), jnp.bfloat16)
    region = region.at[halo : halo + side, halo : halo + side].set(pairs)
    for row_step, column_step in directions:
        from_top, from_bottom = source_span(row_step, side, halo)
        from_left, from_right = source_span(column_step, side, halo)
        moved = passed_along(
            pairs[from_top:from_bottom, from_left:from_right],
            "tile",
            -(row_step * columns + column_step),
        )
        into_top, into_bottom = target_span(row_step, side, halo)
        into_left, into_right = target_span(column_step, side, halo)
        region = region.at[into_top:into_bottom, into_left:into_right].set(moved)
    usable = usable_region(edge_valid[0], grid_row, grid_col, columns, side, halo)
    near = window_mask(band_height, side, halo)
    grads_grid = grad_out.reshape(side, side, local_heads, head_width)
    grad_region = jnp.zeros((width, width, local_heads, 2 * head_width), jnp.float32)
    query_block = queries.reshape(band_height * side, local_heads, head_width)
    grad_block = grads_grid.reshape(band_height * side, local_heads, head_width)
    key_block = region.reshape(-1, local_heads, 2 * head_width)
    allowed = near & usable.reshape(1, -1)
    grad_query, grad_keys, grad_values = band_backward(
        query_block, key_block[:, :, :head_width], key_block[:, :, head_width:], grad_block, allowed
    )
    query_grads = grad_query.reshape(band_height, side, local_heads, head_width)
    joined = jnp.concatenate([grad_keys, grad_values], axis=2).reshape(
        band_height + 2 * halo, width, local_heads, 2 * head_width
    )
    grad_region = grad_region.at[0 : band_height + 2 * halo].add(joined)
    own = grad_region[halo : halo + side, halo : halo + side]
    for row_step, column_step in directions:
        into_top, into_bottom = target_span(row_step, side, halo)
        into_left, into_right = target_span(column_step, side, halo)
        moved = passed_along(
            grad_region[into_top:into_bottom, into_left:into_right].astype(jnp.bfloat16),
            "tile",
            row_step * columns + column_step,
        ).astype(jnp.float32)
        from_top, from_bottom = source_span(row_step, side, halo)
        from_left, from_right = source_span(column_step, side, halo)
        own = own.at[from_top:from_bottom, from_left:from_right].add(moved)
    grad_qkv = (
        jnp.concatenate([query_grads, own], axis=3)
        .reshape(side * side, local_heads * 3 * head_width)
        .astype(jnp.bfloat16)
    )
    grad_w_term = lax.dot_general(
        tokens, grad_qkv, (((0,), (0,)), ((), ())), preferred_element_type=jnp.float32
    ).astype(jnp.bfloat16)
    grad_w = summed_exchange(grad_w_term.reshape(tiles, D // tiles, -1), "tile", None)
    rows = side * side // HEADS
    by_owner = grad_qkv.reshape(HIGH, NEAR, rows, -1).transpose(1, 0, 2, 3).reshape(side * side, -1)
    partial_value = jnp.dot(by_owner, w_qkv, preferred_element_type=jnp.float32)
    near_sum = summed_exchange(
        partial_value.astype(jnp.bfloat16).reshape(NEAR, HIGH * rows, D), "head", near_groups
    )
    grad_x = summed_exchange(
        near_sum.astype(jnp.bfloat16).reshape(HIGH, rows, D), "head", far_groups
    ).astype(jnp.bfloat16)
    return (grad_x, grad_w)


def solution(mesh):
    in_specs = (P("tile", None), P("head", None), P("tile", "head"), P("tile", None))
    out_specs = (P(("tile", "head"), None), P("tile", "head"))
    return jax.shard_map(shards, mesh=mesh, in_specs=in_specs, out_specs=out_specs, check_vma=False)
```

```python
import jax
import jax.numpy as jnp
from jax import lax
from jax.experimental import pallas as pl
from jax.experimental.pallas import tpu as pltpu
from jax.sharding import PartitionSpec as P

D = 1024
HEADS = 16
WIDTH = D // HEADS
HALO = 12
S = 16
GRID_ROWS = 4
GRID_COLS = 8
TILES = 32
OWN = S * S
RIM = HALO * S
COLUMN = OWN + 2 * RIM
NEAR = 4
HIGH = 4
BARRED = -1e30

directions = ((-1, -1), (-1, 0), (-1, 1), (0, -1), (0, 1), (1, -1), (1, 0), (1, 1))
near_groups = [[high * NEAR + near for near in range(NEAR)] for high in range(HIGH)]
far_groups = [[high * NEAR + near for high in range(HIGH)] for near in range(NEAR)]

down_pairs = [(tile, tile + GRID_COLS) for tile in range(TILES - GRID_COLS)]
up_pairs = [(target, source) for source, target in down_pairs]
right_pairs = [(tile, tile + 1) for tile in range(TILES) if tile % GRID_COLS < GRID_COLS - 1]
left_pairs = [(target, source) for source, target in right_pairs]


def summed_exchange(chunks, axis, groups):
    received = lax.all_to_all(chunks, axis, 0, 0, axis_index_groups=groups)
    return jnp.sum(received.astype(jnp.float32), axis=0)


def contract(left, right, left_axis, right_axis):
    return lax.dot_general(
        left, right, (((left_axis,), (right_axis,)), ((), ())), preferred_element_type=jnp.float32
    )


def usable(flags_ref, number, row_step, column_step):
    if (row_step, column_step) == (0, 0):
        return jnp.ones((), jnp.int32)
    grid_row = (number >> 3) + row_step
    grid_col = (number & 7) + column_step
    inside = (grid_row >= 0) & (grid_row < GRID_ROWS) & (grid_col >= 0) & (grid_col < GRID_COLS)
    flag = flags_ref[0, directions.index((row_step, column_step))]
    return jnp.where(inside, flag, 0)


def prepare_kernel(number_ref, flags_ref, tokens_ref, w_ref, query_ref, mask_ref):
    query = contract(w_ref[...], tokens_ref[...], 1, 1).astype(jnp.bfloat16)
    query_ref[:WIDTH, :] = query * jnp.bfloat16(WIDTH**-0.5)
    query_ref[WIDTH : 2 * WIDTH, :] = jnp.zeros((WIDTH, OWN), jnp.bfloat16)
    sublane = lax.broadcasted_iota(jnp.int32, (128, OWN), 0)
    place = lax.broadcasted_iota(jnp.int32, (128, OWN), 1)
    marks = (sublane == (place >> 4)) | (sublane == S + (place & 15)) | (sublane == 2 * S)
    query_ref[2 * WIDTH :, :] = jnp.where(marks, 1.0, 0.0).astype(jnp.bfloat16)
    place = lax.broadcasted_iota(jnp.int32, (COLUMN, 128), 0)
    lane = lax.broadcasted_iota(jnp.int32, (COLUMN, 128), 1)
    key_row = (place >> 4) - HALO
    key_column = place & 15
    far_row = (lane < S) & (jnp.abs(key_row - lane) > HALO)
    column_lane = (lane >= S) & (lane < 2 * S)
    number = number_ref[0]
    for block in range(3):
        offset = key_column + (block - 1) * S - lane + S
        far_column = column_lane & (jnp.abs(offset) > HALO)
        above, beside, below = (usable(flags_ref, number, step, block - 1) for step in (-1, 0, 1))
        flag = jnp.where(key_row < 0, above, jnp.where(key_row >= S, below, beside))
        closed = (lane == 2 * S) & (flag == 0)
        barred = jnp.where(far_row | far_column | closed, BARRED, 0.0)
        mask_ref[block] = barred.astype(jnp.bfloat16)


def prepare(number, flags, tokens, w_qkv):
    whole = lambda shape: pl.BlockSpec(shape, lambda i: (0,) * len(shape))
    return pl.pallas_call(
        prepare_kernel,
        grid=(1,),
        in_specs=[
            pl.BlockSpec(memory_space=pltpu.SMEM),
            pl.BlockSpec(memory_space=pltpu.SMEM),
            whole((OWN, D)),
            whole((WIDTH, D)),
        ],
        out_specs=[whole((256, OWN)), whole((3, COLUMN, 128))],
        out_shape=[
            jax.ShapeDtypeStruct((256, OWN), jnp.bfloat16),
            jax.ShapeDtypeStruct((3, COLUMN, 128), jnp.bfloat16),
        ],
        compiler_params=pltpu.CompilerParams(vmem_limit_bytes=8 << 20),
        name="prepare",
    )(number, flags, tokens, w_qkv)


def attend_kernel(
    query_ref, grad_ref, mask_ref, left_ref, centre_ref, right_ref,
    dquery_ref, dleft_ref, dcentre_ref, dright_ref, scores_ref, low_ref,
):
    pairs = (left_ref, centre_ref, right_ref)
    query = query_ref[...]
    grad = jnp.concatenate([jnp.zeros((WIDTH, OWN), jnp.bfloat16), grad_ref[...]], axis=0)
    highest = None
    for block in range(3):
        rows = pl.ds(block * COLUMN, COLUMN)
        keys = jnp.concatenate([pairs[block][...], mask_ref[block]], axis=1)
        scores = contract(keys, query, 1, 0)
        scores_ref[rows, :] = scores
        top = jnp.max(scores, axis=0, keepdims=True)
        highest = top if highest is None else jnp.maximum(highest, top)
    total = jnp.zeros((1, OWN), jnp.float32)
    for block in range(3):
        rows = pl.ds(block * COLUMN, COLUMN)
        lifted = jnp.exp(scores_ref[rows, :] - highest)
        scores_ref[rows, :] = lifted
        total = total + jnp.sum(lifted, axis=0, keepdims=True)
    inverse = 1.0 / total
    attended = jnp.zeros((128, OWN), jnp.float32)
    for block in range(3):
        rows = pl.ds(block * COLUMN, COLUMN)
        probs = scores_ref[rows, :] * inverse
        scores_ref[rows, :] = probs
        low = probs.astype(jnp.bfloat16)
        low_ref[rows, :] = low
        attended = attended + contract(pairs[block][...], low, 0, 0)
    row_dot = jnp.sum(attended * grad.astype(jnp.float32), axis=0, keepdims=True)
    dquery = jnp.zeros((128, OWN), jnp.float32)
    for block, out_ref in enumerate((dleft_ref, dcentre_ref, dright_ref)):
        rows = pl.ds(block * COLUMN, COLUMN)
        pair = pairs[block][...]
        grad_probs = contract(pair, grad, 1, 0)
        grad_scores = (scores_ref[rows, :] * (grad_probs - row_dot)).astype(jnp.bfloat16)
        dpair = contract(grad_scores, query[:128], 1, 1) + contract(low_ref[rows, :], grad, 1, 1)
        out_ref[...] = dpair.astype(out_ref.dtype)
        dquery = dquery + contract(pair, grad_scores, 0, 0)
    dquery_ref[...] = (dquery[:WIDTH] * WIDTH**-0.5).astype(dquery_ref.dtype)


def attend(query, grad_turned, mask, left, centre, right):
    vmem = pl.BlockSpec(memory_space=pltpu.VMEM)
    return pl.pallas_call(
        attend_kernel,
        in_specs=[vmem] * 6,
        out_specs=[vmem] * 4,
        out_shape=[
            jax.ShapeDtypeStruct((WIDTH, OWN), jnp.bfloat16),
            jax.ShapeDtypeStruct((COLUMN, 128), jnp.bfloat16),
            jax.ShapeDtypeStruct((COLUMN, 128), jnp.float32),
            jax.ShapeDtypeStruct((COLUMN, 128), jnp.bfloat16),
        ],
        scratch_shapes=[
            pltpu.VMEM((3 * COLUMN, OWN), jnp.float32),
            pltpu.VMEM((3 * COLUMN, OWN), jnp.bfloat16),
        ],
        compiler_params=pltpu.CompilerParams(vmem_limit_bytes=16 << 20),
        name="attend",
    )(query, grad_turned, mask, left, centre, right)


def shards(tokens, w_qkv, grad_out, edge_valid):
    number = lax.axis_index("tile")
    pair = contract(tokens, w_qkv[WIDTH:], 1, 1).astype(jnp.bfloat16)
    above = lax.ppermute(pair[OWN - RIM :], "tile", down_pairs)
    below = lax.ppermute(pair[:RIM], "tile", up_pairs)
    query, mask = prepare(number.reshape(1), edge_valid, tokens, w_qkv)
    centre = jnp.concatenate([above, pair, below], axis=0)
    left = lax.ppermute(centre, "tile", right_pairs)
    right = lax.ppermute(centre, "tile", left_pairs)
    dquery, dleft, dcentre, dright = attend(
        query, jnp.transpose(grad_out), mask, left, centre, right
    )
    from_right = lax.ppermute(dleft, "tile", left_pairs)
    from_left = lax.ppermute(dright, "tile", right_pairs)
    column = dcentre + from_right.astype(jnp.float32) + from_left.astype(jnp.float32)
    from_below = lax.ppermute(column[:RIM].astype(jnp.bfloat16), "tile", up_pairs)
    from_above = lax.ppermute(column[OWN + RIM :].astype(jnp.bfloat16), "tile", down_pairs)
    own = (
        column[RIM : RIM + OWN]
        + jnp.pad(from_below.astype(jnp.float32), ((OWN - RIM, 0), (0, 0)))
        + jnp.pad(from_above.astype(jnp.float32), ((0, OWN - RIM), (0, 0)))
    )
    grad_qkv = jnp.concatenate([jnp.transpose(dquery), own.astype(jnp.bfloat16)], axis=1)
    grad_w_term = contract(tokens, grad_qkv, 0, 0).astype(jnp.bfloat16)
    grad_w = summed_exchange(grad_w_term.reshape(TILES, D // TILES, -1), "tile", None)
    rows = OWN // HEADS
    by_owner = grad_qkv.reshape(HIGH, NEAR, rows, -1).transpose(1, 0, 2, 3).reshape(OWN, -1)
    partial_value = contract(by_owner, w_qkv, 1, 0).astype(jnp.bfloat16)
    near_sum = summed_exchange(partial_value.reshape(NEAR, HIGH * rows, D), "head", near_groups)
    grad_x = summed_exchange(
        near_sum.astype(jnp.bfloat16).reshape(HIGH, rows, D), "head", far_groups
    ).astype(jnp.bfloat16)
    return (grad_x, grad_w)


def solution(mesh):
    in_specs = (P("tile", None), P("head", None), P("tile", "head"), P("tile", None))
    out_specs = (P(("tile", "head"), None), P("tile", "head"))
    return jax.shard_map(shards, mesh=mesh, in_specs=in_specs, out_specs=out_specs, check_vma=False)
```

```python
import jax
import jax.numpy as jnp
from jax import lax
from jax.experimental import pallas as pl
from jax.experimental.pallas import tpu as pltpu
from jax.sharding import PartitionSpec as P

D = 1024
HEADS = 16
WIDTH = D // HEADS
HALO = 12
S = 16
GRID_ROWS = 4
GRID_COLS = 8
TILES = 32
OWN = S * S
RIM = HALO * S
COLUMN = OWN + 2 * RIM
NEAR = 4
HIGH = 4
BARRED = -1e30

directions = ((-1, -1), (-1, 0), (-1, 1), (0, -1), (0, 1), (1, -1), (1, 0), (1, 1))
down_pairs = [(tile, tile + GRID_COLS) for tile in range(TILES - GRID_COLS)]
up_pairs = [(target, source) for source, target in down_pairs]
right_pairs = [(tile, tile + 1) for tile in range(TILES) if tile % GRID_COLS < GRID_COLS - 1]
left_pairs = [(target, source) for source, target in right_pairs]


def contract(left, right, left_axis, right_axis):
    return lax.dot_general(
        left, right, (((left_axis,), (right_axis,)), ((), ())), preferred_element_type=jnp.float32
    )


def usable(flags_ref, number, row_step, column_step):
    if (row_step, column_step) == (0, 0):
        return jnp.ones((), jnp.int32)
    grid_row = (number >> 3) + row_step
    grid_col = (number & 7) + column_step
    inside = (grid_row >= 0) & (grid_row < GRID_ROWS) & (grid_col >= 0) & (grid_col < GRID_COLS)
    flag = flags_ref[0, directions.index((row_step, column_step))]
    return jnp.where(inside, flag, 0)


def prepare_kernel(number_ref, flags_ref, tokens_ref, w_ref, query_ref, mask_ref):
    query = contract(w_ref[...], tokens_ref[...], 1, 1).astype(jnp.bfloat16)
    query_ref[:WIDTH, :] = query * jnp.bfloat16(WIDTH**-0.5)
    query_ref[WIDTH : 2 * WIDTH, :] = jnp.zeros((WIDTH, OWN), jnp.bfloat16)
    sublane = lax.broadcasted_iota(jnp.int32, (128, OWN), 0)
    place = lax.broadcasted_iota(jnp.int32, (128, OWN), 1)
    marks = (sublane == (place >> 4)) | (sublane == S + (place & 15)) | (sublane == 2 * S)
    query_ref[2 * WIDTH :, :] = jnp.where(marks, 1.0, 0.0).astype(jnp.bfloat16)
    place = lax.broadcasted_iota(jnp.int32, (COLUMN, 128), 0)
    lane = lax.broadcasted_iota(jnp.int32, (COLUMN, 128), 1)
    key_row = (place >> 4) - HALO
    key_column = place & 15
    far_row = (lane < S) & (jnp.abs(key_row - lane) > HALO)
    column_lane = (lane >= S) & (lane < 2 * S)
    number = number_ref[0]
    for block in range(3):
        offset = key_column + (block - 1) * S - lane + S
        far_column = column_lane & (jnp.abs(offset) > HALO)
        above, beside, below = (usable(flags_ref, number, step, block - 1) for step in (-1, 0, 1))
        flag = jnp.where(key_row < 0, above, jnp.where(key_row >= S, below, beside))
        closed = (lane == 2 * S) & (flag == 0)
        barred = jnp.where(far_row | far_column | closed, BARRED, 0.0)
        mask_ref[block] = barred.astype(jnp.bfloat16)


def prepare(number, flags, tokens, w_qkv):
    whole = lambda shape: pl.BlockSpec(shape, lambda i: (0,) * len(shape))
    return pl.pallas_call(
        prepare_kernel,
        grid=(1,),
        in_specs=[
            pl.BlockSpec(memory_space=pltpu.SMEM),
            pl.BlockSpec(memory_space=pltpu.SMEM),
            whole((OWN, D)),
            whole((WIDTH, D)),
        ],
        out_specs=[whole((256, OWN)), whole((3, COLUMN, 128))],
        out_shape=[
            jax.ShapeDtypeStruct((256, OWN), jnp.bfloat16),
            jax.ShapeDtypeStruct((3, COLUMN, 128), jnp.bfloat16),
        ],
        compiler_params=pltpu.CompilerParams(vmem_limit_bytes=8 << 20),
        name="prepare",
    )(number, flags, tokens, w_qkv)


def attend_kernel(
    query_ref, grad_ref, mask_ref, left_ref, centre_ref, right_ref,
    dquery_ref, dleft_ref, dcentre_ref, dright_ref, scores_ref, low_ref,
):
    pairs = (left_ref, centre_ref, right_ref)
    query = query_ref[...]
    grad = jnp.concatenate([jnp.zeros((WIDTH, OWN), jnp.bfloat16), grad_ref[...]], axis=0)
    highest = None
    for block in range(3):
        rows = pl.ds(block * COLUMN, COLUMN)
        keys = jnp.concatenate([pairs[block][...], mask_ref[block]], axis=1)
        scores = contract(keys, query, 1, 0)
        scores_ref[rows, :] = scores
        top = jnp.max(scores, axis=0, keepdims=True)
        highest = top if highest is None else jnp.maximum(highest, top)
    total = jnp.zeros((1, OWN), jnp.float32)
    for block in range(3):
        rows = pl.ds(block * COLUMN, COLUMN)
        lifted = jnp.exp(scores_ref[rows, :] - highest)
        scores_ref[rows, :] = lifted
        total = total + jnp.sum(lifted, axis=0, keepdims=True)
    inverse = 1.0 / total
    attended = jnp.zeros((128, OWN), jnp.float32)
    for block in range(3):
        rows = pl.ds(block * COLUMN, COLUMN)
        probs = scores_ref[rows, :] * inverse
        scores_ref[rows, :] = probs
        low = probs.astype(jnp.bfloat16)
        low_ref[rows, :] = low
        attended = attended + contract(pairs[block][...], low, 0, 0)
    row_dot = jnp.sum(attended * grad.astype(jnp.float32), axis=0, keepdims=True)
    dquery = jnp.zeros((128, OWN), jnp.float32)
    for block, out_ref in enumerate((dleft_ref, dcentre_ref, dright_ref)):
        rows = pl.ds(block * COLUMN, COLUMN)
        pair = pairs[block][...]
        grad_probs = contract(pair, grad, 1, 0)
        grad_scores = (scores_ref[rows, :] * (grad_probs - row_dot)).astype(jnp.bfloat16)
        dpair = contract(grad_scores, query[:128], 1, 1) + contract(low_ref[rows, :], grad, 1, 1)
        out_ref[...] = dpair.astype(out_ref.dtype)
        dquery = dquery + contract(pair, grad_scores, 0, 0)
    dquery_ref[...] = jnp.transpose(dquery[:WIDTH] * WIDTH**-0.5).astype(dquery_ref.dtype)


def attend(query, grad_turned, mask, left, centre, right):
    vmem = pl.BlockSpec(memory_space=pltpu.VMEM)
    return pl.pallas_call(
        attend_kernel,
        in_specs=[vmem] * 6,
        out_specs=[vmem] * 4,
        out_shape=[
            jax.ShapeDtypeStruct((OWN, WIDTH), jnp.bfloat16),
            jax.ShapeDtypeStruct((COLUMN, 128), jnp.bfloat16),
            jax.ShapeDtypeStruct((COLUMN, 128), jnp.float32),
            jax.ShapeDtypeStruct((COLUMN, 128), jnp.bfloat16),
        ],
        scratch_shapes=[
            pltpu.VMEM((3 * COLUMN, OWN), jnp.float32),
            pltpu.VMEM((3 * COLUMN, OWN), jnp.bfloat16),
        ],
        compiler_params=pltpu.CompilerParams(vmem_limit_bytes=16 << 20),
        name="attend",
    )(query, grad_turned, mask, left, centre, right)


def return_kernel(
    near_ref, column_ref, below_ref, above_ref, dquery_ref, w_ref,
    dqkv_ref, kept_ref, first_ref, second_ref, third_ref, sum_ref, rows_ref,
):
    sum_ref[...] = column_ref[RIM : RIM + OWN]
    sum_ref[OWN - RIM :] += below_ref[...].astype(jnp.float32)
    sum_ref[:RIM] += above_ref[...].astype(jnp.float32)
    dqkv = jnp.concatenate([dquery_ref[...], sum_ref[...].astype(jnp.bfloat16)], axis=1)
    dqkv_ref[...] = dqkv
    rows_ref[...] = dqkv.reshape(HEADS, S, 3 * WIDTH)
    near = near_ref[0]
    w = w_ref[...]
    for step, out_ref in enumerate((kept_ref, first_ref, second_ref, third_ref)):
        target = near ^ step
        chosen = jnp.concatenate([rows_ref[high * NEAR + target] for high in range(HIGH)], axis=0)
        out_ref[...] = contract(chosen, w, 1, 0).astype(jnp.bfloat16)


def project_back(near, column, from_below, from_above, dquery, w_qkv):
    vmem = pl.BlockSpec(memory_space=pltpu.VMEM)
    part = jax.ShapeDtypeStruct((OWN // NEAR, D), jnp.bfloat16)
    return pl.pallas_call(
        return_kernel,
        in_specs=[pl.BlockSpec(memory_space=pltpu.SMEM)] + [vmem] * 5,
        out_specs=[vmem] * 5,
        out_shape=[jax.ShapeDtypeStruct((OWN, 3 * WIDTH), jnp.bfloat16)] + [part] * 4,
        scratch_shapes=[
            pltpu.VMEM((OWN, 128), jnp.float32),
            pltpu.VMEM((HEADS, S, 3 * WIDTH), jnp.bfloat16),
        ],
        compiler_params=pltpu.CompilerParams(vmem_limit_bytes=8 << 20),
        name="project_back",
    )(near, column, from_below, from_above, dquery, w_qkv)


def weight_kernel(turned_ref, dqkv_ref, out_ref):
    out_ref[...] = contract(turned_ref[...], dqkv_ref[...], 1, 0).astype(jnp.bfloat16)


def weight_term(turned, dqkv):
    vmem = pl.BlockSpec(memory_space=pltpu.VMEM)
    return pl.pallas_call(
        weight_kernel,
        in_specs=[vmem] * 2,
        out_specs=vmem,
        out_shape=jax.ShapeDtypeStruct((D, 3 * WIDTH), jnp.bfloat16),
        compiler_params=pltpu.CompilerParams(vmem_limit_bytes=8 << 20),
        name="weight_term",
    )(turned, dqkv)


def near_kernel(high_ref, *refs):
    parts, outs, sum_ref = refs[:NEAR], refs[NEAR : NEAR + HIGH], refs[-1]
    total = sum(part[...].astype(jnp.float32) for part in parts)
    sum_ref[...] = total.astype(jnp.bfloat16).reshape(HIGH, S, D)
    for step, out_ref in enumerate(outs):
        out_ref[...] = sum_ref[high_ref[0] ^ step]


def near_total(high, parts):
    vmem = pl.BlockSpec(memory_space=pltpu.VMEM)
    return pl.pallas_call(
        near_kernel,
        in_specs=[pl.BlockSpec(memory_space=pltpu.SMEM)] + [vmem] * NEAR,
        out_specs=[vmem] * HIGH,
        out_shape=[jax.ShapeDtypeStruct((S, D), jnp.bfloat16)] * HIGH,
        scratch_shapes=[pltpu.VMEM((HIGH, S, D), jnp.bfloat16)],
        compiler_params=pltpu.CompilerParams(vmem_limit_bytes=8 << 20),
        name="near_total",
    )(high, *parts)


def near_swap(step):
    return [(head, head ^ step) for head in range(HEADS)]


def far_swap(step):
    return [(head, head ^ (step * NEAR)) for head in range(HEADS)]


def shards(tokens, w_qkv, grad_out, edge_valid):
    number = lax.axis_index("tile")
    head = lax.axis_index("head")
    near, high = head & (NEAR - 1), head >> 2
    pair = contract(tokens, w_qkv[WIDTH:], 1, 1).astype(jnp.bfloat16)
    above = lax.ppermute(pair[OWN - RIM :], "tile", down_pairs)
    below = lax.ppermute(pair[:RIM], "tile", up_pairs)
    query, mask = prepare(number.reshape(1), edge_valid, tokens, w_qkv)
    above, below, query, mask = lax.optimization_barrier((above, below, query, mask))
    turned = jnp.transpose(tokens)
    centre = jnp.concatenate([above, pair, below], axis=0)
    left = lax.ppermute(centre, "tile", right_pairs)
    right = lax.ppermute(centre, "tile", left_pairs)
    left, right, turned = lax.optimization_barrier((left, right, turned))
    dquery, dleft, dcentre, dright = attend(
        query, jnp.transpose(grad_out), mask, left, centre, right
    )
    from_right = lax.ppermute(dleft, "tile", left_pairs)
    from_left = lax.ppermute(dright, "tile", right_pairs)
    column = dcentre + from_right.astype(jnp.float32) + from_left.astype(jnp.float32)
    from_below = lax.ppermute(column[:RIM].astype(jnp.bfloat16), "tile", up_pairs)
    from_above = lax.ppermute(column[OWN + RIM :].astype(jnp.bfloat16), "tile", down_pairs)
    dqkv, *parts = project_back(
        near.reshape(1), column, from_below, from_above, dquery, w_qkv
    )
    for step in (2, 1, 3):
        parts[step] = lax.ppermute(parts[step], "head", near_swap(step))
    term = weight_term(turned, dqkv)
    terms = lax.all_to_all(term.reshape(TILES, D // TILES, -1), "tile", 0, 0)
    chunks = list(near_total(high.reshape(1), parts))
    for step in (3, 2, 1):
        chunks[step] = lax.ppermute(chunks[step], "head", far_swap(step))
    grad_x = sum(chunk.astype(jnp.float32) for chunk in chunks).astype(jnp.bfloat16)
    grad_w = jnp.sum(terms.astype(jnp.float32), axis=0)
    return (grad_x, grad_w)


def solution(mesh):
    in_specs = (P("tile", None), P("head", None), P("tile", "head"), P("tile", None))
    out_specs = (P(("tile", "head"), None), P("tile", "head"))
    return jax.shard_map(shards, mesh=mesh, in_specs=in_specs, out_specs=out_specs, check_vma=False)
```

```python
import jax
import jax.numpy as jnp
from jax import lax
from jax.experimental import pallas as pl
from jax.experimental.pallas import tpu as pltpu
from jax.sharding import PartitionSpec as P

D = 1024
HEADS = 16
WIDTH = D // HEADS
HALO = 12
S = 16
GRID_ROWS = 4
GRID_COLS = 8
TILES = 32
OWN = S * S
RIM = HALO * S
COLUMN = OWN + 2 * RIM
NEAR = 4
HIGH = 4
BARRED = -1e30

directions = ((-1, -1), (-1, 0), (-1, 1), (0, -1), (0, 1), (1, -1), (1, 0), (1, 1))
down_pairs = [(tile, tile + GRID_COLS) for tile in range(TILES - GRID_COLS)]
up_pairs = [(target, source) for source, target in down_pairs]
twin_pairs = [(tile, tile ^ 1) for tile in range(TILES)]
next_pairs = [
    (tile, tile + 2 * (tile & 1) - 1)
    for tile in range(TILES)
    if 0 <= tile % GRID_COLS + 2 * (tile & 1) - 1 < GRID_COLS
]


def contract(left, right, left_axis, right_axis):
    return lax.dot_general(
        left, right, (((left_axis,), (right_axis,)), ((), ())), preferred_element_type=jnp.float32
    )


def usable(flags_ref, number, row_step, column_step):
    if (row_step, column_step) == (0, 0):
        return jnp.ones((), jnp.int32)
    grid_row = (number >> 3) + row_step
    grid_col = (number & 7) + column_step
    inside = (grid_row >= 0) & (grid_row < GRID_ROWS) & (grid_col >= 0) & (grid_col < GRID_COLS)
    flag = flags_ref[0, directions.index((row_step, column_step))]
    return jnp.where(inside, flag, 0)


def prepare_kernel(number_ref, flags_ref, tokens_ref, w_ref, query_ref, mask_ref):
    query = contract(w_ref[...], tokens_ref[...], 1, 1).astype(jnp.bfloat16)
    query_ref[:WIDTH, :] = query * jnp.bfloat16(WIDTH**-0.5)
    query_ref[WIDTH : 2 * WIDTH, :] = jnp.zeros((WIDTH, OWN), jnp.bfloat16)
    sublane = lax.broadcasted_iota(jnp.int32, (128, OWN), 0)
    place = lax.broadcasted_iota(jnp.int32, (128, OWN), 1)
    marks = (sublane == (place >> 4)) | (sublane == S + (place & 15)) | (sublane == 2 * S)
    query_ref[2 * WIDTH :, :] = jnp.where(marks, 1.0, 0.0).astype(jnp.bfloat16)
    place = lax.broadcasted_iota(jnp.int32, (COLUMN, 128), 0)
    lane = lax.broadcasted_iota(jnp.int32, (COLUMN, 128), 1)
    key_row = (place >> 4) - HALO
    key_column = place & 15
    far_row = (lane < S) & (jnp.abs(key_row - lane) > HALO)
    column_lane = (lane >= S) & (lane < 2 * S)
    number = number_ref[0]
    odd = number & 1
    for block in range(3):
        column_step = (block - 1) * (1 - 2 * odd)
        offset = key_column + column_step * S - lane + S
        far_column = column_lane & (jnp.abs(offset) > HALO)
        above, beside, below = (
            jnp.where(
                odd == 1,
                usable(flags_ref, number, step, 1 - block),
                usable(flags_ref, number, step, block - 1),
            )
            for step in (-1, 0, 1)
        )
        flag = jnp.where(key_row < 0, above, jnp.where(key_row >= S, below, beside))
        closed = (lane == 2 * S) & (flag == 0)
        barred = jnp.where(far_row | far_column | closed, BARRED, 0.0)
        mask_ref[block] = barred.astype(jnp.bfloat16)


def prepare(number, flags, tokens, w_qkv):
    whole = lambda shape: pl.BlockSpec(shape, lambda i: (0,) * len(shape))
    return pl.pallas_call(
        prepare_kernel,
        grid=(1,),
        in_specs=[
            pl.BlockSpec(memory_space=pltpu.SMEM),
            pl.BlockSpec(memory_space=pltpu.SMEM),
            whole((OWN, D)),
            whole((WIDTH, D)),
        ],
        out_specs=[whole((256, OWN)), whole((3, COLUMN, 128))],
        out_shape=[
            jax.ShapeDtypeStruct((256, OWN), jnp.bfloat16),
            jax.ShapeDtypeStruct((3, COLUMN, 128), jnp.bfloat16),
        ],
        compiler_params=pltpu.CompilerParams(vmem_limit_bytes=8 << 20),
        name="prepare",
    )(number, flags, tokens, w_qkv)


def attend_kernel(
    query_ref, grad_ref, mask_ref, left_ref, centre_ref, right_ref,
    dquery_ref, dleft_ref, dcentre_ref, dright_ref, scores_ref, low_ref,
):
    pairs = (left_ref, centre_ref, right_ref)
    query = query_ref[...]
    grad = jnp.concatenate([jnp.zeros((WIDTH, OWN), jnp.bfloat16), grad_ref[...]], axis=0)
    highest = None
    for block in range(3):
        rows = pl.ds(block * COLUMN, COLUMN)
        keys = jnp.concatenate([pairs[block][...], mask_ref[block]], axis=1)
        scores = contract(keys, query, 1, 0)
        scores_ref[rows, :] = scores
        top = jnp.max(scores, axis=0, keepdims=True)
        highest = top if highest is None else jnp.maximum(highest, top)
    total = jnp.zeros((1, OWN), jnp.float32)
    for block in range(3):
        rows = pl.ds(block * COLUMN, COLUMN)
        lifted = jnp.exp(scores_ref[rows, :] - highest)
        scores_ref[rows, :] = lifted
        total = total + jnp.sum(lifted, axis=0, keepdims=True)
    inverse = 1.0 / total
    attended = jnp.zeros((128, OWN), jnp.float32)
    for block in range(3):
        rows = pl.ds(block * COLUMN, COLUMN)
        probs = scores_ref[rows, :] * inverse
        scores_ref[rows, :] = probs
        low = probs.astype(jnp.bfloat16)
        low_ref[rows, :] = low
        attended = attended + contract(pairs[block][...], low, 0, 0)
    row_dot = jnp.sum(attended * grad.astype(jnp.float32), axis=0, keepdims=True)
    dquery = jnp.zeros((128, OWN), jnp.float32)
    for block, out_ref in enumerate((dleft_ref, dcentre_ref, dright_ref)):
        rows = pl.ds(block * COLUMN, COLUMN)
        pair = pairs[block][...]
        grad_probs = contract(pair, grad, 1, 0)
        grad_scores = (scores_ref[rows, :] * (grad_probs - row_dot)).astype(jnp.bfloat16)
        dpair = contract(grad_scores, query[:128], 1, 1) + contract(low_ref[rows, :], grad, 1, 1)
        out_ref[...] = dpair.astype(out_ref.dtype)
        dquery = dquery + contract(pair, grad_scores, 0, 0)
    dquery_ref[...] = jnp.transpose(dquery[:WIDTH] * WIDTH**-0.5).astype(dquery_ref.dtype)


def attend(query, grad_turned, mask, left, centre, right):
    vmem = pl.BlockSpec(memory_space=pltpu.VMEM)
    return pl.pallas_call(
        attend_kernel,
        in_specs=[vmem] * 6,
        out_specs=[vmem] * 4,
        out_shape=[
            jax.ShapeDtypeStruct((OWN, WIDTH), jnp.bfloat16),
            jax.ShapeDtypeStruct((COLUMN, 128), jnp.bfloat16),
            jax.ShapeDtypeStruct((COLUMN, 128), jnp.float32),
            jax.ShapeDtypeStruct((COLUMN, 128), jnp.bfloat16),
        ],
        scratch_shapes=[
            pltpu.VMEM((3 * COLUMN, OWN), jnp.float32),
            pltpu.VMEM((3 * COLUMN, OWN), jnp.bfloat16),
        ],
        compiler_params=pltpu.CompilerParams(vmem_limit_bytes=16 << 20),
        name="attend",
    )(query, grad_turned, mask, left, centre, right)


def return_kernel(
    near_ref, column_ref, below_ref, above_ref, dquery_ref, w_ref,
    dqkv_ref, kept_ref, first_ref, second_ref, third_ref, sum_ref, rows_ref,
):
    sum_ref[...] = column_ref[RIM : RIM + OWN]
    sum_ref[OWN - RIM :] += below_ref[...].astype(jnp.float32)
    sum_ref[:RIM] += above_ref[...].astype(jnp.float32)
    dqkv = jnp.concatenate([dquery_ref[...], sum_ref[...].astype(jnp.bfloat16)], axis=1)
    dqkv_ref[...] = dqkv
    rows_ref[...] = dqkv.reshape(HEADS, S, 3 * WIDTH)
    near = near_ref[0]
    w = w_ref[...]
    for step, out_ref in enumerate((kept_ref, first_ref, second_ref, third_ref)):
        target = near ^ step
        chosen = jnp.concatenate([rows_ref[high * NEAR + target] for high in range(HIGH)], axis=0)
        out_ref[...] = contract(chosen, w, 1, 0).astype(jnp.bfloat16)


def project_back(near, column, from_below, from_above, dquery, w_qkv):
    vmem = pl.BlockSpec(memory_space=pltpu.VMEM)
    part = jax.ShapeDtypeStruct((OWN // NEAR, D), jnp.bfloat16)
    return pl.pallas_call(
        return_kernel,
        in_specs=[pl.BlockSpec(memory_space=pltpu.SMEM)] + [vmem] * 5,
        out_specs=[vmem] * 5,
        out_shape=[jax.ShapeDtypeStruct((OWN, 3 * WIDTH), jnp.bfloat16)] + [part] * 4,
        scratch_shapes=[
            pltpu.VMEM((OWN, 128), jnp.float32),
            pltpu.VMEM((HEADS, S, 3 * WIDTH), jnp.bfloat16),
        ],
        compiler_params=pltpu.CompilerParams(vmem_limit_bytes=8 << 20),
        name="project_back",
    )(near, column, from_below, from_above, dquery, w_qkv)


def weight_kernel(turned_ref, dqkv_ref, out_ref):
    out_ref[...] = contract(turned_ref[...], dqkv_ref[...], 1, 0).astype(jnp.bfloat16)


def weight_term(turned, dqkv):
    vmem = pl.BlockSpec(memory_space=pltpu.VMEM)
    return pl.pallas_call(
        weight_kernel,
        in_specs=[vmem] * 2,
        out_specs=vmem,
        out_shape=jax.ShapeDtypeStruct((D, 3 * WIDTH), jnp.bfloat16),
        compiler_params=pltpu.CompilerParams(vmem_limit_bytes=8 << 20),
        name="weight_term",
    )(turned, dqkv)


def near_kernel(high_ref, *refs):
    parts, outs, sum_ref = refs[:NEAR], refs[NEAR : NEAR + HIGH], refs[-1]
    total = sum(part[...].astype(jnp.float32) for part in parts)
    sum_ref[...] = total.astype(jnp.bfloat16).reshape(HIGH, S, D)
    for step, out_ref in enumerate(outs):
        out_ref[...] = sum_ref[high_ref[0] ^ step]


def near_total(high, parts):
    vmem = pl.BlockSpec(memory_space=pltpu.VMEM)
    return pl.pallas_call(
        near_kernel,
        in_specs=[pl.BlockSpec(memory_space=pltpu.SMEM)] + [vmem] * NEAR,
        out_specs=[vmem] * HIGH,
        out_shape=[jax.ShapeDtypeStruct((S, D), jnp.bfloat16)] * HIGH,
        scratch_shapes=[pltpu.VMEM((HIGH, S, D), jnp.bfloat16)],
        compiler_params=pltpu.CompilerParams(vmem_limit_bytes=8 << 20),
        name="near_total",
    )(high, *parts)


def near_swap(step):
    return [(head, head ^ step) for head in range(HEADS)]


def far_swap(step):
    return [(head, head ^ (step * NEAR)) for head in range(HEADS)]


def local_step(tokens, w_qkv, grad_out, edge_valid):
    number = lax.axis_index("tile")
    head = lax.axis_index("head")
    near, high = head & (NEAR - 1), head >> 2
    pair = contract(tokens, w_qkv[WIDTH:], 1, 1).astype(jnp.bfloat16)
    above = lax.ppermute(pair[OWN - RIM :], "tile", down_pairs)
    below = lax.ppermute(pair[:RIM], "tile", up_pairs)
    query, mask = prepare(number.reshape(1), edge_valid, tokens, w_qkv)
    above, below, query, mask = lax.optimization_barrier((above, below, query, mask))
    turned = jnp.transpose(tokens)
    centre = jnp.concatenate([above, pair, below], axis=0)
    beyond = lax.ppermute(centre, "tile", next_pairs)
    twin = lax.ppermute(centre, "tile", twin_pairs)
    beyond, twin, turned = lax.optimization_barrier((beyond, twin, turned))
    dquery, dbeyond, dcentre, dtwin = attend(
        query, jnp.transpose(grad_out), mask, beyond, centre, twin
    )
    from_beyond = lax.ppermute(dbeyond, "tile", next_pairs)
    from_twin = lax.ppermute(dtwin, "tile", twin_pairs)
    column = dcentre + from_beyond.astype(jnp.float32) + from_twin.astype(jnp.float32)
    from_below = lax.ppermute(column[:RIM].astype(jnp.bfloat16), "tile", up_pairs)
    from_above = lax.ppermute(column[OWN + RIM :].astype(jnp.bfloat16), "tile", down_pairs)
    dqkv, *parts = project_back(near.reshape(1), column, from_below, from_above, dquery, w_qkv)
    for step in (2, 1, 3):
        parts[step] = lax.ppermute(parts[step], "head", near_swap(step))
    term = weight_term(turned, dqkv)
    terms = lax.all_to_all(term.reshape(TILES, D // TILES, -1), "tile", 0, 0)
    chunks = list(near_total(high.reshape(1), parts))
    for step in (2, 1, 3):
        chunks[step] = lax.ppermute(chunks[step], "head", far_swap(step))
    grad_w = jnp.sum(terms.astype(jnp.float32), axis=0)
    grad_x = sum(chunk.astype(jnp.float32) for chunk in chunks).astype(jnp.bfloat16)
    return (grad_x, grad_w)


def solution(mesh):
    in_specs = (P("tile", None), P("head", None), P("tile", "head"), P("tile", None))
    out_specs = (P(("tile", "head"), None), P("tile", "head"))
    return jax.shard_map(local_step, mesh=mesh, in_specs=in_specs, out_specs=out_specs, check_vma=False)
```

```python
import jax
import jax.numpy as jnp
from jax import lax
from jax.experimental import pallas as pl
from jax.experimental.pallas import tpu as pltpu
from jax.sharding import PartitionSpec as P

D = 1024
HEADS = 16
WIDTH = D // HEADS
HALO = 12
S = 16
GRID_ROWS = 4
GRID_COLS = 8
TILES = 32
OWN = S * S
RIM = HALO * S
COLUMN = OWN + 2 * RIM
NEAR = 4
HIGH = 4
BARRED = -1e30

directions = ((-1, -1), (-1, 0), (-1, 1), (0, -1), (0, 1), (1, -1), (1, 0), (1, 1))
down_pairs = [(tile, tile + GRID_COLS) for tile in range(TILES - GRID_COLS)]
up_pairs = [(target, source) for source, target in down_pairs]
twin_pairs = [(tile, tile ^ 1) for tile in range(TILES)]
next_pairs = [
    (tile, tile + 2 * (tile & 1) - 1)
    for tile in range(TILES)
    if 0 <= tile % GRID_COLS + 2 * (tile & 1) - 1 < GRID_COLS
]


def contract(left, right, left_axis, right_axis):
    return lax.dot_general(
        left, right, (((left_axis,), (right_axis,)), ((), ())), preferred_element_type=jnp.float32
    )


def usable(flags_ref, number, row_step, column_step):
    if (row_step, column_step) == (0, 0):
        return jnp.ones((), jnp.int32)
    grid_row = (number >> 3) + row_step
    grid_col = (number & 7) + column_step
    inside = (grid_row >= 0) & (grid_row < GRID_ROWS) & (grid_col >= 0) & (grid_col < GRID_COLS)
    flag = flags_ref[0, directions.index((row_step, column_step))]
    return jnp.where(inside, flag, 0)


def prepare_kernel(number_ref, flags_ref, tokens_ref, w_ref, query_ref, mask_ref):
    query = contract(w_ref[...], tokens_ref[...], 1, 1).astype(jnp.bfloat16)
    query_ref[:WIDTH, :] = query * jnp.bfloat16(WIDTH**-0.5)
    query_ref[WIDTH : 2 * WIDTH, :] = jnp.zeros((WIDTH, OWN), jnp.bfloat16)
    sublane = lax.broadcasted_iota(jnp.int32, (128, OWN), 0)
    place = lax.broadcasted_iota(jnp.int32, (128, OWN), 1)
    marks = (sublane == (place >> 4)) | (sublane == S + (place & 15)) | (sublane == 2 * S)
    query_ref[2 * WIDTH :, :] = jnp.where(marks, 1.0, 0.0).astype(jnp.bfloat16)
    place = lax.broadcasted_iota(jnp.int32, (COLUMN, 128), 0)
    lane = lax.broadcasted_iota(jnp.int32, (COLUMN, 128), 1)
    key_row = (place >> 4) - HALO
    key_column = place & 15
    far_row = (lane < S) & (jnp.abs(key_row - lane) > HALO)
    column_lane = (lane >= S) & (lane < 2 * S)
    number = number_ref[0]
    odd = number & 1
    for block in range(3):
        column_step = (block - 1) * (1 - 2 * odd)
        offset = key_column + column_step * S - lane + S
        far_column = column_lane & (jnp.abs(offset) > HALO)
        above, beside, below = (
            jnp.where(
                odd == 1,
                usable(flags_ref, number, step, 1 - block),
                usable(flags_ref, number, step, block - 1),
            )
            for step in (-1, 0, 1)
        )
        flag = jnp.where(key_row < 0, above, jnp.where(key_row >= S, below, beside))
        closed = (lane == 2 * S) & (flag == 0)
        barred = jnp.where(far_row | far_column | closed, BARRED, 0.0)
        mask_ref[block] = barred.astype(jnp.bfloat16)


def prepare(number, flags, tokens, w_qkv):
    whole = lambda shape: pl.BlockSpec(shape, lambda i: (0,) * len(shape))
    return pl.pallas_call(
        prepare_kernel,
        grid=(1,),
        in_specs=[
            pl.BlockSpec(memory_space=pltpu.SMEM),
            pl.BlockSpec(memory_space=pltpu.SMEM),
            whole((OWN, D)),
            whole((WIDTH, D)),
        ],
        out_specs=[whole((256, OWN)), whole((3, COLUMN, 128))],
        out_shape=[
            jax.ShapeDtypeStruct((256, OWN), jnp.bfloat16),
            jax.ShapeDtypeStruct((3, COLUMN, 128), jnp.bfloat16),
        ],
        compiler_params=pltpu.CompilerParams(vmem_limit_bytes=8 << 20),
        name="prepare",
    )(number, flags, tokens, w_qkv)


def attend_kernel(
    query_ref, grad_ref, mask_ref, left_ref, centre_ref, right_ref,
    dquery_ref, dleft_ref, dcentre_ref, dright_ref, scores_ref, low_ref,
):
    pairs = (left_ref, centre_ref, right_ref)
    query = query_ref[...]
    grad = jnp.concatenate([jnp.zeros((WIDTH, OWN), jnp.bfloat16), grad_ref[...]], axis=0)
    highest = None
    for block in range(3):
        rows = pl.ds(block * COLUMN, COLUMN)
        keys = jnp.concatenate([pairs[block][...], mask_ref[block]], axis=1)
        scores = contract(keys, query, 1, 0)
        scores_ref[rows, :] = scores
        top = jnp.max(scores, axis=0, keepdims=True)
        highest = top if highest is None else jnp.maximum(highest, top)
    total = jnp.zeros((1, OWN), jnp.float32)
    for block in range(3):
        rows = pl.ds(block * COLUMN, COLUMN)
        lifted = jnp.exp(scores_ref[rows, :] - highest)
        scores_ref[rows, :] = lifted
        total = total + jnp.sum(lifted, axis=0, keepdims=True)
    inverse = 1.0 / total
    attended = jnp.zeros((128, OWN), jnp.float32)
    for block in range(3):
        rows = pl.ds(block * COLUMN, COLUMN)
        probs = scores_ref[rows, :] * inverse
        scores_ref[rows, :] = probs
        low = probs.astype(jnp.bfloat16)
        low_ref[rows, :] = low
        attended = attended + contract(pairs[block][...], low, 0, 0)
    row_dot = jnp.sum(attended * grad.astype(jnp.float32), axis=0, keepdims=True)
    dquery = jnp.zeros((128, OWN), jnp.float32)
    for block, out_ref in enumerate((dleft_ref, dcentre_ref, dright_ref)):
        rows = pl.ds(block * COLUMN, COLUMN)
        pair = pairs[block][...]
        grad_probs = contract(pair, grad, 1, 0)
        grad_scores = (scores_ref[rows, :] * (grad_probs - row_dot)).astype(jnp.bfloat16)
        dpair = contract(grad_scores, query[:128], 1, 1) + contract(low_ref[rows, :], grad, 1, 1)
        out_ref[...] = dpair.astype(out_ref.dtype)
        dquery = dquery + contract(pair, grad_scores, 0, 0)
    dquery_ref[...] = jnp.transpose(dquery[:WIDTH] * WIDTH**-0.5).astype(dquery_ref.dtype)


def attend(query, grad_turned, mask, left, centre, right):
    vmem = pl.BlockSpec(memory_space=pltpu.VMEM)
    return pl.pallas_call(
        attend_kernel,
        in_specs=[vmem] * 6,
        out_specs=[vmem] * 4,
        out_shape=[
            jax.ShapeDtypeStruct((OWN, WIDTH), jnp.bfloat16),
            jax.ShapeDtypeStruct((COLUMN, 128), jnp.bfloat16),
            jax.ShapeDtypeStruct((COLUMN, 128), jnp.float32),
            jax.ShapeDtypeStruct((COLUMN, 128), jnp.bfloat16),
        ],
        scratch_shapes=[
            pltpu.VMEM((3 * COLUMN, OWN), jnp.float32),
            pltpu.VMEM((3 * COLUMN, OWN), jnp.bfloat16),
        ],
        compiler_params=pltpu.CompilerParams(vmem_limit_bytes=16 << 20),
        name="attend",
    )(query, grad_turned, mask, left, centre, right)


def return_kernel(
    near_ref, column_ref, below_ref, above_ref, dquery_ref, w_ref,
    dqkv_ref, kept_ref, first_ref, second_ref, third_ref, sum_ref, rows_ref,
):
    sum_ref[...] = column_ref[RIM : RIM + OWN]
    sum_ref[OWN - RIM :] += below_ref[...].astype(jnp.float32)
    sum_ref[:RIM] += above_ref[...].astype(jnp.float32)
    dqkv = jnp.concatenate([dquery_ref[...], sum_ref[...].astype(jnp.bfloat16)], axis=1)
    dqkv_ref[...] = dqkv
    rows_ref[...] = dqkv.reshape(HEADS, S, 3 * WIDTH)
    near = near_ref[0]
    w = w_ref[...]
    for step, out_ref in enumerate((kept_ref, first_ref, second_ref, third_ref)):
        target = near ^ step
        chosen = jnp.concatenate([rows_ref[high * NEAR + target] for high in range(HIGH)], axis=0)
        out_ref[...] = contract(chosen, w, 1, 0).astype(jnp.bfloat16)


def project_back(near, column, from_below, from_above, dquery, w_qkv):
    vmem = pl.BlockSpec(memory_space=pltpu.VMEM)
    part = jax.ShapeDtypeStruct((OWN // NEAR, D), jnp.bfloat16)
    return pl.pallas_call(
        return_kernel,
        in_specs=[pl.BlockSpec(memory_space=pltpu.SMEM)] + [vmem] * 5,
        out_specs=[vmem] * 5,
        out_shape=[jax.ShapeDtypeStruct((OWN, 3 * WIDTH), jnp.bfloat16)] + [part] * 4,
        scratch_shapes=[
            pltpu.VMEM((OWN, 128), jnp.float32),
            pltpu.VMEM((HEADS, S, 3 * WIDTH), jnp.bfloat16),
        ],
        compiler_params=pltpu.CompilerParams(vmem_limit_bytes=8 << 20),
        name="project_back",
    )(near, column, from_below, from_above, dquery, w_qkv)


def weight_kernel(turned_ref, dqkv_ref, out_ref):
    out_ref[...] = contract(turned_ref[...], dqkv_ref[...], 1, 0).astype(jnp.bfloat16)


def weight_term(turned, dqkv):
    vmem = pl.BlockSpec(memory_space=pltpu.VMEM)
    return pl.pallas_call(
        weight_kernel,
        in_specs=[vmem] * 2,
        out_specs=vmem,
        out_shape=jax.ShapeDtypeStruct((D, 3 * WIDTH), jnp.bfloat16),
        compiler_params=pltpu.CompilerParams(vmem_limit_bytes=8 << 20),
        name="weight_term",
    )(turned, dqkv)


def near_kernel(high_ref, *refs):
    parts, outs, sum_ref = refs[:NEAR], refs[NEAR:-1], refs[-1]
    total = sum(part[...].astype(jnp.float32) for part in parts)
    sum_ref[...] = total.astype(jnp.bfloat16).reshape(HIGH, S, D)
    for step, out_ref in zip((0, -1, 1, 2), outs):
        out_ref[...] = sum_ref[(high_ref[0] + step) & (HIGH - 1)]


def near_total(high, parts):
    vmem = pl.BlockSpec(memory_space=pltpu.VMEM)
    return pl.pallas_call(
        near_kernel,
        in_specs=[pl.BlockSpec(memory_space=pltpu.SMEM)] + [vmem] * NEAR,
        out_specs=[vmem] * HIGH,
        out_shape=[jax.ShapeDtypeStruct((S, D), jnp.bfloat16)] * HIGH,
        scratch_shapes=[pltpu.VMEM((HIGH, S, D), jnp.bfloat16)],
        compiler_params=pltpu.CompilerParams(vmem_limit_bytes=8 << 20),
        name="near_total",
    )(high, *parts)


def tile_kernel(terms_ref, out_ref):
    out_ref[...] = jnp.sum(terms_ref[...].astype(jnp.float32), axis=0)


def tile_total(terms):
    vmem = pl.BlockSpec(memory_space=pltpu.VMEM)
    return pl.pallas_call(
        tile_kernel,
        in_specs=[vmem],
        out_specs=vmem,
        out_shape=jax.ShapeDtypeStruct((D // TILES, 3 * WIDTH), jnp.float32),
        compiler_params=pltpu.CompilerParams(vmem_limit_bytes=8 << 20),
        name="tile_total",
    )(terms)


def near_swap(step):
    return [(head, head ^ step) for head in range(HEADS)]


def far_moves(*blocks):
    return [(a * NEAR + near, b * NEAR + near) for a, b in blocks for near in range(NEAR)]


def local_step(tokens, w_qkv, grad_out, edge_valid):
    number = lax.axis_index("tile")
    head = lax.axis_index("head")
    near, high = head & (NEAR - 1), head >> 2
    pair = contract(tokens, w_qkv[WIDTH:], 1, 1).astype(jnp.bfloat16)
    above = lax.ppermute(pair[OWN - RIM :], "tile", down_pairs)
    below = lax.ppermute(pair[:RIM], "tile", up_pairs)
    query, mask = prepare(number.reshape(1), edge_valid, tokens, w_qkv)
    above, below, query, mask = lax.optimization_barrier((above, below, query, mask))
    turned = jnp.transpose(tokens)
    centre = jnp.concatenate([above, pair, below], axis=0)
    beyond = lax.ppermute(centre, "tile", next_pairs)
    twin = lax.ppermute(centre, "tile", twin_pairs)
    beyond, twin, turned = lax.optimization_barrier((beyond, twin, turned))
    dquery, dbeyond, dcentre, dtwin = attend(
        query, jnp.transpose(grad_out), mask, beyond, centre, twin
    )
    from_beyond = lax.ppermute(dbeyond, "tile", next_pairs)
    from_twin = lax.ppermute(dtwin, "tile", twin_pairs)
    column = dcentre + from_beyond.astype(jnp.float32) + from_twin.astype(jnp.float32)
    from_below = lax.ppermute(column[:RIM].astype(jnp.bfloat16), "tile", up_pairs)
    from_above = lax.ppermute(column[OWN + RIM :].astype(jnp.bfloat16), "tile", down_pairs)
    dqkv, *parts = project_back(near.reshape(1), column, from_below, from_above, dquery, w_qkv)
    for step in (2, 1, 3):
        parts[step] = lax.ppermute(parts[step], "head", near_swap(step))
    term = weight_term(turned, dqkv)
    terms = lax.all_to_all(term.reshape(TILES, D // TILES, -1), "tile", 0, 0)
    kept, before, after, across = near_total(high.reshape(1), parts)
    chunks = [
        kept,
        lax.ppermute(before, "head", far_moves((1, 0), (2, 1))),
        lax.ppermute(after, "head", far_moves((3, 0))),
        lax.ppermute(across, "head", far_moves((0, 2), (1, 3), (2, 0), (3, 1))),
        lax.ppermute(after, "head", far_moves((0, 1), (1, 2), (2, 3))),
        lax.ppermute(before, "head", far_moves((3, 2), (0, 3))),
    ]
    grad_w = tile_total(terms)
    grad_x = sum(chunk.astype(jnp.float32) for chunk in chunks).astype(jnp.bfloat16)
    return (grad_x, grad_w)


def solution(mesh):
    in_specs = (P("tile", None), P("head", None), P("tile", "head"), P("tile", None))
    out_specs = (P(("tile", "head"), None), P("tile", "head"))
    return jax.shard_map(local_step, mesh=mesh, in_specs=in_specs, out_specs=out_specs, check_vma=False)
```

```python
import jax
import jax.numpy as jnp
from jax import lax
from jax.experimental import pallas as pl
from jax.experimental.pallas import tpu as pltpu
from jax.sharding import PartitionSpec as P

D = 1024
HEADS = 16
WIDTH = D // HEADS
HALO = 12
S = 16
GRID_ROWS = 4
GRID_COLS = 8
TILES = 32
OWN = S * S
RIM = HALO * S
COLUMN = OWN + 2 * RIM
NEAR = 4
HIGH = 4
BARRED = -1e30

directions = ((-1, -1), (-1, 0), (-1, 1), (0, -1), (0, 1), (1, -1), (1, 0), (1, 1))
fold_pairs = [(tile, tile ^ GRID_COLS) for tile in range(TILES)]
middle_pairs = [
    (tile, tile ^ (3 * GRID_COLS)) for tile in range(TILES) if 0 < tile // GRID_COLS < GRID_ROWS - 1
]
twin_pairs = [(tile, tile ^ 1) for tile in range(TILES)]
next_pairs = [
    (tile, tile + 2 * (tile & 1) - 1)
    for tile in range(TILES)
    if 0 <= tile % GRID_COLS + 2 * (tile & 1) - 1 < GRID_COLS
]


def contract(left, right, left_axis, right_axis):
    return lax.dot_general(
        left, right, (((left_axis,), (right_axis,)), ((), ())), preferred_element_type=jnp.float32
    )


def usable(flags_ref, number, row_step, column_step):
    if (row_step, column_step) == (0, 0):
        return jnp.ones((), jnp.int32)
    grid_row = (number >> 3) + row_step
    grid_col = (number & 7) + column_step
    inside = (grid_row >= 0) & (grid_row < GRID_ROWS) & (grid_col >= 0) & (grid_col < GRID_COLS)
    flag = flags_ref[0, directions.index((row_step, column_step))]
    return jnp.where(inside, flag, 0)


def prepare_kernel(number_ref, flags_ref, tokens_ref, w_ref, query_ref, mask_ref):
    query = contract(w_ref[...], tokens_ref[...], 1, 1).astype(jnp.bfloat16)
    query_ref[:WIDTH, :] = query * jnp.bfloat16(WIDTH**-0.5)
    query_ref[WIDTH : 2 * WIDTH, :] = jnp.zeros((WIDTH, OWN), jnp.bfloat16)
    sublane = lax.broadcasted_iota(jnp.int32, (128, OWN), 0)
    place = lax.broadcasted_iota(jnp.int32, (128, OWN), 1)
    marks = (sublane == (place >> 4)) | (sublane == S + (place & 15)) | (sublane == 2 * S)
    query_ref[2 * WIDTH :, :] = jnp.where(marks, 1.0, 0.0).astype(jnp.bfloat16)
    place = lax.broadcasted_iota(jnp.int32, (COLUMN, 128), 0)
    lane = lax.broadcasted_iota(jnp.int32, (COLUMN, 128), 1)
    key_row = (place >> 4) - HALO
    key_column = place & 15
    far_row = (lane < S) & (jnp.abs(key_row - lane) > HALO)
    column_lane = (lane >= S) & (lane < 2 * S)
    number = number_ref[0]
    odd = number & 1
    for block in range(3):
        column_step = (block - 1) * (1 - 2 * odd)
        offset = key_column + column_step * S - lane + S
        far_column = column_lane & (jnp.abs(offset) > HALO)
        above, beside, below = (
            jnp.where(
                odd == 1,
                usable(flags_ref, number, step, 1 - block),
                usable(flags_ref, number, step, block - 1),
            )
            for step in (-1, 0, 1)
        )
        flag = jnp.where(key_row < 0, above, jnp.where(key_row >= S, below, beside))
        closed = (lane == 2 * S) & (flag == 0)
        barred = jnp.where(far_row | far_column | closed, BARRED, 0.0)
        mask_ref[block] = barred.astype(jnp.bfloat16)


def prepare(number, flags, tokens, w_qkv):
    whole = lambda shape: pl.BlockSpec(shape, lambda i: (0,) * len(shape))
    return pl.pallas_call(
        prepare_kernel,
        grid=(1,),
        in_specs=[
            pl.BlockSpec(memory_space=pltpu.SMEM),
            pl.BlockSpec(memory_space=pltpu.SMEM),
            whole((OWN, D)),
            whole((WIDTH, D)),
        ],
        out_specs=[whole((256, OWN)), whole((3, COLUMN, 128))],
        out_shape=[
            jax.ShapeDtypeStruct((256, OWN), jnp.bfloat16),
            jax.ShapeDtypeStruct((3, COLUMN, 128), jnp.bfloat16),
        ],
        compiler_params=pltpu.CompilerParams(vmem_limit_bytes=8 << 20),
        name="prepare",
    )(number, flags, tokens, w_qkv)


def attend_kernel(
    query_ref, grad_ref, mask_ref, beyond_ref, centre_ref, twin_ref,
    dbeyond_ref, dtwin_ref, probs_ref, probs_low_ref, row_dot_ref, dquery_ref,
    scores_ref, low_ref,
):
    pairs = (beyond_ref, centre_ref, twin_ref)
    query = query_ref[...]
    grad = jnp.concatenate([jnp.zeros((WIDTH, OWN), jnp.bfloat16), grad_ref[...]], axis=0)
    highest = None
    for block in range(3):
        rows = pl.ds(block * COLUMN, COLUMN)
        keys = jnp.concatenate([pairs[block][...], mask_ref[block]], axis=1)
        scores = contract(keys, query, 1, 0)
        scores_ref[rows, :] = scores
        top = jnp.max(scores, axis=0, keepdims=True)
        highest = top if highest is None else jnp.maximum(highest, top)
    total = jnp.zeros((1, OWN), jnp.float32)
    for block in range(3):
        rows = pl.ds(block * COLUMN, COLUMN)
        lifted = jnp.exp(scores_ref[rows, :] - highest)
        scores_ref[rows, :] = lifted
        total = total + jnp.sum(lifted, axis=0, keepdims=True)
    inverse = 1.0 / total
    attended = jnp.zeros((128, OWN), jnp.float32)
    for block in range(3):
        rows = pl.ds(block * COLUMN, COLUMN)
        probs = scores_ref[rows, :] * inverse
        scores_ref[rows, :] = probs
        low = probs.astype(jnp.bfloat16)
        low_ref[rows, :] = low
        attended = attended + contract(pairs[block][...], low, 0, 0)
    row_dot = jnp.sum(attended * grad.astype(jnp.float32), axis=0, keepdims=True)
    dquery = jnp.zeros((128, OWN), jnp.float32)
    for block, out_ref in ((0, dbeyond_ref), (2, dtwin_ref)):
        rows = pl.ds(block * COLUMN, COLUMN)
        dpair, dquery = block_backward(
            pairs[block][...], query, grad, scores_ref[rows, :], low_ref[rows, :], row_dot, dquery
        )
        out_ref[...] = dpair.astype(jnp.bfloat16)
    probs_ref[...] = scores_ref[COLUMN : 2 * COLUMN, :]
    probs_low_ref[...] = low_ref[COLUMN : 2 * COLUMN, :]
    row_dot_ref[...] = row_dot
    dquery_ref[...] = dquery


def block_backward(pair, query, grad, probs, low, row_dot, dquery):
    grad_probs = contract(pair, grad, 1, 0)
    grad_scores = (probs * (grad_probs - row_dot)).astype(jnp.bfloat16)
    dpair = contract(grad_scores, query[:128], 1, 1) + contract(low, grad, 1, 1)
    return dpair, dquery + contract(pair, grad_scores, 0, 0)


def attend(query, grad_turned, mask, beyond, centre, twin):
    vmem = pl.BlockSpec(memory_space=pltpu.VMEM)
    return pl.pallas_call(
        attend_kernel,
        in_specs=[vmem] * 6,
        out_specs=[vmem] * 6,
        out_shape=[
            jax.ShapeDtypeStruct((COLUMN, 128), jnp.bfloat16),
            jax.ShapeDtypeStruct((COLUMN, 128), jnp.bfloat16),
            jax.ShapeDtypeStruct((COLUMN, OWN), jnp.float32),
            jax.ShapeDtypeStruct((COLUMN, OWN), jnp.bfloat16),
            jax.ShapeDtypeStruct((1, OWN), jnp.float32),
            jax.ShapeDtypeStruct((128, OWN), jnp.float32),
        ],
        scratch_shapes=[
            pltpu.VMEM((3 * COLUMN, OWN), jnp.float32),
            pltpu.VMEM((3 * COLUMN, OWN), jnp.bfloat16),
        ],
        compiler_params=pltpu.CompilerParams(vmem_limit_bytes=16 << 20),
        name="attend",
    )(query, grad_turned, mask, beyond, centre, twin)


def finish_kernel(
    query_ref, grad_ref, centre_ref, probs_ref, low_ref, row_dot_ref, dquery_ref,
    out_query_ref, out_pair_ref,
):
    grad = jnp.concatenate([jnp.zeros((WIDTH, OWN), jnp.bfloat16), grad_ref[...]], axis=0)
    dpair, dquery = block_backward(
        centre_ref[...], query_ref[...], grad, probs_ref[...], low_ref[...], row_dot_ref[...],
        dquery_ref[...],
    )
    out_pair_ref[...] = dpair
    out_query_ref[...] = jnp.transpose(dquery[:WIDTH] * WIDTH**-0.5).astype(jnp.bfloat16)


def finish(query, grad_turned, centre, probs, low, row_dot, dquery):
    vmem = pl.BlockSpec(memory_space=pltpu.VMEM)
    return pl.pallas_call(
        finish_kernel,
        in_specs=[vmem] * 7,
        out_specs=[vmem] * 2,
        out_shape=[
            jax.ShapeDtypeStruct((OWN, WIDTH), jnp.bfloat16),
            jax.ShapeDtypeStruct((COLUMN, 128), jnp.float32),
        ],
        compiler_params=pltpu.CompilerParams(vmem_limit_bytes=16 << 20),
        name="finish",
    )(query, grad_turned, centre, probs, low, row_dot, dquery)


def return_kernel(
    near_ref, odd_ref, column_ref, fold_ref, middle_ref, dquery_ref, w_ref,
    dqkv_ref, kept_ref, first_ref, second_ref, third_ref, sum_ref, rows_ref,
):
    sum_ref[...] = column_ref[RIM : RIM + OWN]
    odd = odd_ref[0] == 1
    fold = fold_ref[...].astype(jnp.float32)
    middle = middle_ref[...].astype(jnp.float32)
    sum_ref[OWN - RIM :] += jnp.where(odd, middle, fold)
    sum_ref[:RIM] += jnp.where(odd, fold, middle)
    dqkv = jnp.concatenate([dquery_ref[...], sum_ref[...].astype(jnp.bfloat16)], axis=1)
    dqkv_ref[...] = dqkv
    rows_ref[...] = dqkv.reshape(HEADS, S, 3 * WIDTH)
    near = near_ref[0]
    w = w_ref[...]
    for step, out_ref in enumerate((kept_ref, first_ref, second_ref, third_ref)):
        target = near ^ step
        chosen = jnp.concatenate([rows_ref[high * NEAR + target] for high in range(HIGH)], axis=0)
        out_ref[...] = contract(chosen, w, 1, 0).astype(jnp.bfloat16)


def project_back(near, odd, column, from_fold, from_middle, dquery, w_qkv):
    vmem = pl.BlockSpec(memory_space=pltpu.VMEM)
    part = jax.ShapeDtypeStruct((OWN // NEAR, D), jnp.bfloat16)
    return pl.pallas_call(
        return_kernel,
        in_specs=[pl.BlockSpec(memory_space=pltpu.SMEM)] * 2 + [vmem] * 5,
        out_specs=[vmem] * 5,
        out_shape=[jax.ShapeDtypeStruct((OWN, 3 * WIDTH), jnp.bfloat16)] + [part] * 4,
        scratch_shapes=[
            pltpu.VMEM((OWN, 128), jnp.float32),
            pltpu.VMEM((HEADS, S, 3 * WIDTH), jnp.bfloat16),
        ],
        compiler_params=pltpu.CompilerParams(vmem_limit_bytes=8 << 20),
        name="project_back",
    )(near, odd, column, from_fold, from_middle, dquery, w_qkv)


def weight_kernel(turned_ref, dqkv_ref, out_ref):
    out_ref[...] = contract(turned_ref[...], dqkv_ref[...], 1, 0).astype(jnp.bfloat16)


def weight_term(turned, dqkv):
    vmem = pl.BlockSpec(memory_space=pltpu.VMEM)
    return pl.pallas_call(
        weight_kernel,
        in_specs=[vmem] * 2,
        out_specs=vmem,
        out_shape=jax.ShapeDtypeStruct((D, 3 * WIDTH), jnp.bfloat16),
        compiler_params=pltpu.CompilerParams(vmem_limit_bytes=8 << 20),
        name="weight_term",
    )(turned, dqkv)


def near_kernel(high_ref, *refs):
    parts, outs, sum_ref = refs[:NEAR], refs[NEAR:-1], refs[-1]
    total = sum(part[...].astype(jnp.float32) for part in parts)
    sum_ref[...] = total.astype(jnp.bfloat16).reshape(HIGH, S, D)
    for step, out_ref in zip((0, -1, 1, 2), outs):
        out_ref[...] = sum_ref[(high_ref[0] + step) & (HIGH - 1)]


def near_total(high, parts):
    vmem = pl.BlockSpec(memory_space=pltpu.VMEM)
    return pl.pallas_call(
        near_kernel,
        in_specs=[pl.BlockSpec(memory_space=pltpu.SMEM)] + [vmem] * NEAR,
        out_specs=[vmem] * HIGH,
        out_shape=[jax.ShapeDtypeStruct((S, D), jnp.bfloat16)] * HIGH,
        scratch_shapes=[pltpu.VMEM((HIGH, S, D), jnp.bfloat16)],
        compiler_params=pltpu.CompilerParams(vmem_limit_bytes=8 << 20),
        name="near_total",
    )(high, *parts)


def tile_kernel(terms_ref, out_ref):
    out_ref[...] = jnp.sum(terms_ref[...].astype(jnp.float32), axis=0)


def tile_total(terms):
    vmem = pl.BlockSpec(memory_space=pltpu.VMEM)
    return pl.pallas_call(
        tile_kernel,
        in_specs=[vmem],
        out_specs=vmem,
        out_shape=jax.ShapeDtypeStruct((D // TILES, 3 * WIDTH), jnp.float32),
        compiler_params=pltpu.CompilerParams(vmem_limit_bytes=8 << 20),
        name="tile_total",
    )(terms)


def near_swap(step):
    return [(head, head ^ step) for head in range(HEADS)]


def far_moves(*blocks):
    return [(a * NEAR + near, b * NEAR + near) for a, b in blocks for near in range(NEAR)]


def local_step(tokens, w_qkv, grad_out, edge_valid):
    number = lax.axis_index("tile")
    head = lax.axis_index("head")
    near, high = head & (NEAR - 1), head >> 2
    pair = contract(tokens, w_qkv[WIDTH:], 1, 1).astype(jnp.bfloat16)
    odd = (number // GRID_COLS) & 1
    fold = jnp.where(odd == 1, pair[:RIM], pair[OWN - RIM :])
    middle = jnp.where(odd == 1, pair[OWN - RIM :], pair[:RIM])
    fold = lax.ppermute(fold, "tile", fold_pairs)
    middle = lax.ppermute(middle, "tile", middle_pairs)
    query, mask = prepare(number.reshape(1), edge_valid, tokens, w_qkv)
    fold, middle, query, mask = lax.optimization_barrier((fold, middle, query, mask))
    above = jnp.where(odd == 1, fold, middle)
    below = jnp.where(odd == 1, middle, fold)
    turned = jnp.transpose(tokens)
    centre = jnp.concatenate([above, pair, below], axis=0)
    beyond = lax.ppermute(centre, "tile", next_pairs)
    twin = lax.ppermute(centre, "tile", twin_pairs)
    beyond, twin, turned = lax.optimization_barrier((beyond, twin, turned))
    grad_turned = jnp.transpose(grad_out)
    dbeyond, dtwin, *saved = attend(query, grad_turned, mask, beyond, centre, twin)
    from_beyond = lax.ppermute(dbeyond, "tile", next_pairs)
    from_twin = lax.ppermute(dtwin, "tile", twin_pairs)
    dquery, dcentre = finish(query, grad_turned, centre, *saved)
    column = dcentre + from_beyond.astype(jnp.float32) + from_twin.astype(jnp.float32)
    upper = column[:RIM].astype(jnp.bfloat16)
    lower = column[OWN + RIM :].astype(jnp.bfloat16)
    from_fold = lax.ppermute(jnp.where(odd == 1, upper, lower), "tile", fold_pairs)
    from_middle = lax.ppermute(jnp.where(odd == 1, lower, upper), "tile", middle_pairs)
    dqkv, *parts = project_back(
        near.reshape(1), odd.reshape(1), column, from_fold, from_middle, dquery, w_qkv
    )
    for step in (2, 1, 3):
        parts[step] = lax.ppermute(parts[step], "head", near_swap(step))
    term = weight_term(turned, dqkv)
    terms = lax.all_to_all(term.reshape(TILES, D // TILES, -1), "tile", 0, 0)
    kept, before, after, across = near_total(high.reshape(1), parts)
    chunks = [
        kept,
        lax.ppermute(before, "head", far_moves((1, 0), (2, 1))),
        lax.ppermute(after, "head", far_moves((3, 0))),
        lax.ppermute(across, "head", far_moves((0, 2), (1, 3), (2, 0), (3, 1))),
        lax.ppermute(after, "head", far_moves((0, 1), (1, 2), (2, 3))),
        lax.ppermute(before, "head", far_moves((3, 2), (0, 3))),
    ]
    grad_w = tile_total(terms)
    grad_x = sum(chunk.astype(jnp.float32) for chunk in chunks).astype(jnp.bfloat16)
    return (grad_x, grad_w)


def solution(mesh):
    in_specs = (P("tile", None), P("head", None), P("tile", "head"), P("tile", None))
    out_specs = (P(("tile", "head"), None), P("tile", "head"))
    return jax.shard_map(local_step, mesh=mesh, in_specs=in_specs, out_specs=out_specs, check_vma=False)
```

```python
import jax
import jax.numpy as jnp
from jax import lax
from jax.experimental import pallas as pl
from jax.experimental.pallas import tpu as pltpu
from jax.sharding import PartitionSpec as P


D = 1024
HEADS = 16
WIDTH = D // HEADS
HALO = 12
S = 16
GRID_ROWS = 4
GRID_COLS = 8
TILES = 32
OWN = S * S
RIM = HALO * S
COLUMN = OWN + 2 * RIM
NEAR = 4
HIGH = 4
BARRED = -1e30

directions = ((-1, -1), (-1, 0), (-1, 1), (0, -1), (0, 1), (1, -1), (1, 0), (1, 1))
fold_pairs = [(tile, tile ^ GRID_COLS) for tile in range(TILES)]
middle_pairs = [
    (tile, tile ^ (3 * GRID_COLS)) for tile in range(TILES) if 0 < tile // GRID_COLS < GRID_ROWS - 1
]
twin_pairs = [(tile, tile ^ 1) for tile in range(TILES)]
next_pairs = [
    (tile, tile + 2 * (tile & 1) - 1)
    for tile in range(TILES)
    if 0 <= tile % GRID_COLS + 2 * (tile & 1) - 1 < GRID_COLS
]


def contract(left, right, left_axis, right_axis):
    return lax.dot_general(
        left, right, (((left_axis,), (right_axis,)), ((), ())), preferred_element_type=jnp.float32
    )


far_rounds = (
    ((1, 0),),
    ((1, 3), (2, 0), (3, 1)),
    ((0, 2), (3, 0)),
    ((0, 1), (1, 2)),
    ((0, 3), (3, 2), (2, 1)),
    ((2, 3),),
)


core_groups = [[2 * place + core for place in range(TILES // 2)] for core in range(2)]


def usable(flags_ref, number, row_step, column_step):
    if (row_step, column_step) == (0, 0):
        return jnp.ones((), jnp.int32)
    grid_row = (number >> 3) + row_step
    grid_col = (number & 7) + column_step
    inside = (grid_row >= 0) & (grid_row < GRID_ROWS) & (grid_col >= 0) & (grid_col < GRID_COLS)
    flag = flags_ref[0, directions.index((row_step, column_step))]
    return jnp.where(inside, flag, 0)


def prepare_kernel(number_ref, flags_ref, tokens_ref, w_ref, query_ref, mask_ref):
    query = contract(w_ref[...], tokens_ref[...], 1, 1).astype(jnp.bfloat16)
    query_ref[:WIDTH, :] = query * jnp.bfloat16(WIDTH**-0.5)
    query_ref[WIDTH : 2 * WIDTH, :] = jnp.zeros((WIDTH, OWN), jnp.bfloat16)
    sublane = lax.broadcasted_iota(jnp.int32, (128, OWN), 0)
    place = lax.broadcasted_iota(jnp.int32, (128, OWN), 1)
    marks = (sublane == (place >> 4)) | (sublane == S + (place & 15)) | (sublane == 2 * S)
    query_ref[2 * WIDTH :, :] = jnp.where(marks, 1.0, 0.0).astype(jnp.bfloat16)
    place = lax.broadcasted_iota(jnp.int32, (COLUMN, 128), 0)
    lane = lax.broadcasted_iota(jnp.int32, (COLUMN, 128), 1)
    key_row = (place >> 4) - HALO
    key_column = place & 15
    far_row = (lane < S) & (jnp.abs(key_row - lane) > HALO)
    column_lane = (lane >= S) & (lane < 2 * S)
    number = number_ref[0]
    odd = number & 1
    for block in range(3):
        column_step = (block - 1) * (1 - 2 * odd)
        offset = key_column + column_step * S - lane + S
        far_column = column_lane & (jnp.abs(offset) > HALO)
        above, beside, below = (
            jnp.where(
                odd == 1,
                usable(flags_ref, number, step, 1 - block),
                usable(flags_ref, number, step, block - 1),
            )
            for step in (-1, 0, 1)
        )
        flag = jnp.where(key_row < 0, above, jnp.where(key_row >= S, below, beside))
        closed = (lane == 2 * S) & (flag == 0)
        barred = jnp.where(far_row | far_column | closed, BARRED, 0.0)
        mask_ref[block] = barred.astype(jnp.bfloat16)


def prepare(number, flags, tokens, w_qkv):
    whole = lambda shape: pl.BlockSpec(shape, lambda i: (0,) * len(shape))
    return pl.pallas_call(
        prepare_kernel,
        grid=(1,),
        in_specs=[
            pl.BlockSpec(memory_space=pltpu.SMEM),
            pl.BlockSpec(memory_space=pltpu.SMEM),
            whole((OWN, D)),
            whole((WIDTH, D)),
        ],
        out_specs=[whole((256, OWN)), whole((3, COLUMN, 128))],
        out_shape=[
            jax.ShapeDtypeStruct((256, OWN), jnp.bfloat16),
            jax.ShapeDtypeStruct((3, COLUMN, 128), jnp.bfloat16),
        ],
        compiler_params=pltpu.CompilerParams(vmem_limit_bytes=8 << 20),
        name="prepare",
    )(number, flags, tokens, w_qkv)


def early_kernel(query_ref, mask_ref, centre_ref, lifted_ref, top_ref, total_ref):
    keys = jnp.concatenate([centre_ref[...], mask_ref[1]], axis=1)
    scores = contract(keys, query_ref[...], 1, 0)
    top = jnp.max(scores, axis=0, keepdims=True)
    lifted = jnp.exp(scores - top)
    lifted_ref[...] = lifted
    top_ref[...] = top
    total_ref[...] = jnp.sum(lifted, axis=0, keepdims=True)


def centre_scores(query, mask, centre):
    vmem = pl.BlockSpec(memory_space=pltpu.VMEM)
    return pl.pallas_call(
        early_kernel,
        in_specs=[vmem] * 3,
        out_specs=[vmem] * 3,
        out_shape=[
            jax.ShapeDtypeStruct((COLUMN, OWN), jnp.float32),
            jax.ShapeDtypeStruct((1, OWN), jnp.float32),
            jax.ShapeDtypeStruct((1, OWN), jnp.float32),
        ],
        compiler_params=pltpu.CompilerParams(vmem_limit_bytes=8 << 20),
        name="centre_scores",
    )(query, mask, centre)


def attend_kernel(
    query_ref, grad_ref, mask_ref, beyond_ref, centre_ref, twin_ref,
    lifted_ref, top_ref, total_ref,
    dbeyond_ref, dtwin_ref, probs_ref, probs_low_ref, row_dot_ref, dquery_ref,
    scores_ref, low_ref,
):
    query = query_ref[...]
    grad = jnp.concatenate([jnp.zeros((WIDTH, OWN), jnp.bfloat16), grad_ref[...]], axis=0)
    sides = ((beyond_ref, 0, dbeyond_ref), (twin_ref, 2, dtwin_ref))
    own_top = top_ref[...]
    highest = own_top
    for place, (pair_ref, block, _) in enumerate(sides):
        rows = pl.ds(place * COLUMN, COLUMN)
        keys = jnp.concatenate([pair_ref[...], mask_ref[block]], axis=1)
        scores = contract(keys, query, 1, 0)
        scores_ref[rows, :] = scores
        highest = jnp.maximum(highest, jnp.max(scores, axis=0, keepdims=True))
    own_scale = jnp.exp(own_top - highest)
    total = total_ref[...] * own_scale
    for place in range(2):
        rows = pl.ds(place * COLUMN, COLUMN)
        lifted = jnp.exp(scores_ref[rows, :] - highest)
        scores_ref[rows, :] = lifted
        total = total + jnp.sum(lifted, axis=0, keepdims=True)
    inverse = 1.0 / total
    probs = lifted_ref[...] * (own_scale * inverse)
    low = probs.astype(jnp.bfloat16)
    probs_ref[...] = probs
    probs_low_ref[...] = low
    attended = contract(centre_ref[...], low, 0, 0)
    for place, (pair_ref, _, _) in enumerate(sides):
        rows = pl.ds(place * COLUMN, COLUMN)
        probs = scores_ref[rows, :] * inverse
        scores_ref[rows, :] = probs
        low = probs.astype(jnp.bfloat16)
        low_ref[rows, :] = low
        attended = attended + contract(pair_ref[...], low, 0, 0)
    row_dot = jnp.sum(attended * grad.astype(jnp.float32), axis=0, keepdims=True)
    dquery = jnp.zeros((128, OWN), jnp.float32)
    for place, (pair_ref, _, out_ref) in enumerate(sides):
        rows = pl.ds(place * COLUMN, COLUMN)
        dpair, dquery = block_backward(
            pair_ref[...], query, grad, scores_ref[rows, :], low_ref[rows, :], row_dot, dquery
        )
        out_ref[...] = dpair.astype(jnp.bfloat16)
    row_dot_ref[...] = row_dot
    dquery_ref[...] = dquery


def block_backward(pair, query, grad, probs, low, row_dot, dquery):
    grad_probs = contract(pair, grad, 1, 0)
    grad_scores = (probs * (grad_probs - row_dot)).astype(jnp.bfloat16)
    dpair = contract(grad_scores, query[:128], 1, 1) + contract(low, grad, 1, 1)
    return dpair, dquery + contract(pair, grad_scores, 0, 0)


def attend(query, grad_turned, mask, beyond, centre, twin, early):
    vmem = pl.BlockSpec(memory_space=pltpu.VMEM)
    return pl.pallas_call(
        attend_kernel,
        in_specs=[vmem] * 9,
        out_specs=[vmem] * 6,
        out_shape=[
            jax.ShapeDtypeStruct((COLUMN, 128), jnp.bfloat16),
            jax.ShapeDtypeStruct((COLUMN, 128), jnp.bfloat16),
            jax.ShapeDtypeStruct((COLUMN, OWN), jnp.float32),
            jax.ShapeDtypeStruct((COLUMN, OWN), jnp.bfloat16),
            jax.ShapeDtypeStruct((1, OWN), jnp.float32),
            jax.ShapeDtypeStruct((128, OWN), jnp.float32),
        ],
        scratch_shapes=[
            pltpu.VMEM((2 * COLUMN, OWN), jnp.float32),
            pltpu.VMEM((2 * COLUMN, OWN), jnp.bfloat16),
        ],
        compiler_params=pltpu.CompilerParams(vmem_limit_bytes=16 << 20),
        name="attend",
    )(query, grad_turned, mask, beyond, centre, twin, *early)


def finish_kernel(
    query_ref, grad_ref, centre_ref, probs_ref, low_ref, row_dot_ref, dquery_ref,
    out_query_ref, out_pair_ref,
):
    grad = jnp.concatenate([jnp.zeros((WIDTH, OWN), jnp.bfloat16), grad_ref[...]], axis=0)
    dpair, dquery = block_backward(
        centre_ref[...], query_ref[...], grad, probs_ref[...], low_ref[...], row_dot_ref[...],
        dquery_ref[...],
    )
    out_pair_ref[...] = dpair
    out_query_ref[...] = jnp.transpose(dquery[:WIDTH] * WIDTH**-0.5).astype(jnp.bfloat16)


def finish(query, grad_turned, centre, probs, low, row_dot, dquery):
    vmem = pl.BlockSpec(memory_space=pltpu.VMEM)
    return pl.pallas_call(
        finish_kernel,
        in_specs=[vmem] * 7,
        out_specs=[vmem] * 2,
        out_shape=[
            jax.ShapeDtypeStruct((OWN, WIDTH), jnp.bfloat16),
            jax.ShapeDtypeStruct((COLUMN, 128), jnp.float32),
        ],
        compiler_params=pltpu.CompilerParams(vmem_limit_bytes=16 << 20),
        name="finish",
    )(query, grad_turned, centre, probs, low, row_dot, dquery)


def return_kernel(
    near_ref, odd_ref, column_ref, fold_ref, middle_ref, dquery_ref, w_ref,
    dqkv_ref, kept_ref, first_ref, second_ref, third_ref, sum_ref, rows_ref,
):
    sum_ref[...] = column_ref[RIM : RIM + OWN]
    odd = odd_ref[0] == 1
    fold = fold_ref[...].astype(jnp.float32)
    middle = middle_ref[...].astype(jnp.float32)
    sum_ref[OWN - RIM :] += jnp.where(odd, middle, fold)
    sum_ref[:RIM] += jnp.where(odd, fold, middle)
    dqkv = jnp.concatenate([dquery_ref[...], sum_ref[...].astype(jnp.bfloat16)], axis=1)
    dqkv_ref[...] = dqkv
    rows_ref[...] = dqkv.reshape(HEADS, S, 3 * WIDTH)
    near = near_ref[0]
    w = w_ref[...]
    for step, out_ref in enumerate((kept_ref, first_ref, second_ref, third_ref)):
        target = near ^ step
        chosen = jnp.concatenate([rows_ref[high * NEAR + target] for high in range(HIGH)], axis=0)
        out_ref[...] = contract(chosen, w, 1, 0).astype(jnp.bfloat16)


def project_back(near, odd, column, from_fold, from_middle, dquery, w_qkv):
    vmem = pl.BlockSpec(memory_space=pltpu.VMEM)
    part = jax.ShapeDtypeStruct((OWN // NEAR, D), jnp.bfloat16)
    return pl.pallas_call(
        return_kernel,
        in_specs=[pl.BlockSpec(memory_space=pltpu.SMEM)] * 2 + [vmem] * 5,
        out_specs=[vmem] * 5,
        out_shape=[jax.ShapeDtypeStruct((OWN, 3 * WIDTH), jnp.bfloat16)] + [part] * 4,
        scratch_shapes=[
            pltpu.VMEM((OWN, 128), jnp.float32),
            pltpu.VMEM((HEADS, S, 3 * WIDTH), jnp.bfloat16),
        ],
        compiler_params=pltpu.CompilerParams(vmem_limit_bytes=8 << 20),
        name="project_back",
    )(near, odd, column, from_fold, from_middle, dquery, w_qkv)


def weight_kernel(turned_ref, lent_ref, dqkv_ref, twin_ref, out_ref):
    term = contract(turned_ref[...], dqkv_ref[...], 1, 0)
    out_ref[...] = (term + contract(lent_ref[...], twin_ref[...], 1, 0)).astype(jnp.bfloat16)


def weight_term(turned, lent, dqkv, twin):
    vmem = pl.BlockSpec(memory_space=pltpu.VMEM)
    return pl.pallas_call(
        weight_kernel,
        in_specs=[vmem] * 4,
        out_specs=vmem,
        out_shape=jax.ShapeDtypeStruct((D // 2, 3 * WIDTH), jnp.bfloat16),
        compiler_params=pltpu.CompilerParams(vmem_limit_bytes=8 << 20),
        name="weight_term",
    )(turned, lent, dqkv, twin)


def near_kernel(high_ref, *refs):
    parts, outs, sum_ref = refs[:NEAR], refs[NEAR:-1], refs[-1]
    total = sum(part[...].astype(jnp.float32) for part in parts)
    sum_ref[...] = total.astype(jnp.bfloat16).reshape(HIGH, S, D)
    high = high_ref[0]
    outs[0][...] = sum_ref[high]
    for moves, out_ref in zip(far_rounds, outs[1:]):
        target = 0
        for source, sent in moves:
            target = jnp.where(high == source, sent, target)
        out_ref[...] = sum_ref[target]


def near_total(high, parts):
    vmem = pl.BlockSpec(memory_space=pltpu.VMEM)
    outs = 1 + len(far_rounds)
    return pl.pallas_call(
        near_kernel,
        in_specs=[pl.BlockSpec(memory_space=pltpu.SMEM)] + [vmem] * NEAR,
        out_specs=[vmem] * outs,
        out_shape=[jax.ShapeDtypeStruct((S, D), jnp.bfloat16)] * outs,
        scratch_shapes=[pltpu.VMEM((HIGH, S, D), jnp.bfloat16)],
        compiler_params=pltpu.CompilerParams(vmem_limit_bytes=8 << 20),
        name="near_total",
    )(high, *parts)


def tile_kernel(terms_ref, out_ref):
    out_ref[...] = jnp.sum(terms_ref[...].astype(jnp.float32), axis=0)


def tile_total(terms):
    vmem = pl.BlockSpec(memory_space=pltpu.VMEM)
    return pl.pallas_call(
        tile_kernel,
        in_specs=[vmem],
        out_specs=vmem,
        out_shape=jax.ShapeDtypeStruct((D // TILES, 3 * WIDTH), jnp.float32),
        compiler_params=pltpu.CompilerParams(vmem_limit_bytes=8 << 20),
        name="tile_total",
    )(terms)


def near_swap(step):
    return [(head, head ^ step) for head in range(HEADS)]


def far_moves(*blocks):
    return [(a * NEAR + near, b * NEAR + near) for a, b in blocks for near in range(NEAR)]


def local_step(tokens, w_qkv, grad_out, edge_valid):
    number = lax.axis_index("tile")
    head = lax.axis_index("head")
    near, high = head & (NEAR - 1), head >> 2
    pair = contract(tokens, w_qkv[WIDTH:], 1, 1).astype(jnp.bfloat16)
    odd = (number // GRID_COLS) & 1
    fold = jnp.where(odd == 1, pair[:RIM], pair[OWN - RIM :])
    middle = jnp.where(odd == 1, pair[OWN - RIM :], pair[:RIM])
    fold = lax.ppermute(fold, "tile", fold_pairs)
    middle = lax.ppermute(middle, "tile", middle_pairs)
    query, mask = prepare(number.reshape(1), edge_valid, tokens, w_qkv)
    fold, middle, query, mask = lax.optimization_barrier((fold, middle, query, mask))
    above = jnp.where(odd == 1, fold, middle)
    below = jnp.where(odd == 1, middle, fold)
    core = number & 1
    turned = jnp.transpose(tokens).reshape(TILES // 2, 2, D // TILES, OWN)
    kept_rows = lax.dynamic_index_in_dim(turned, core, 1, False).reshape(D // 2, OWN)
    lent_rows = lax.dynamic_index_in_dim(turned, 1 - core, 1, False).reshape(D // 2, OWN)
    centre = jnp.concatenate([above, pair, below], axis=0)
    beyond = lax.ppermute(centre, "tile", next_pairs)
    twin = lax.ppermute(centre, "tile", twin_pairs)
    early = centre_scores(query, mask, centre)
    beyond, twin, kept_rows, lent_rows = lax.optimization_barrier(
        (beyond, twin, kept_rows, lent_rows)
    )
    grad_turned = jnp.transpose(grad_out)
    dbeyond, dtwin, *saved = attend(query, grad_turned, mask, beyond, centre, twin, early)
    from_beyond = lax.ppermute(dbeyond, "tile", next_pairs)
    from_twin = lax.ppermute(dtwin, "tile", twin_pairs)
    dquery, dcentre = finish(query, grad_turned, centre, *saved)
    column = dcentre + from_beyond.astype(jnp.float32) + from_twin.astype(jnp.float32)
    upper = column[:RIM].astype(jnp.bfloat16)
    lower = column[OWN + RIM :].astype(jnp.bfloat16)
    from_fold = lax.ppermute(jnp.where(odd == 1, upper, lower), "tile", fold_pairs)
    from_middle = lax.ppermute(jnp.where(odd == 1, lower, upper), "tile", middle_pairs)
    lent_rows = lax.ppermute(lent_rows, "tile", twin_pairs)
    dqkv, *parts = project_back(
        near.reshape(1), odd.reshape(1), column, from_fold, from_middle, dquery, w_qkv
    )
    twin_dqkv = lax.ppermute(dqkv, "tile", twin_pairs)
    for step in (2, 1, 3):
        parts[step] = lax.ppermute(parts[step], "head", near_swap(step))
    term = weight_term(kept_rows, lent_rows, dqkv, twin_dqkv)
    terms = lax.all_to_all(
        term.reshape(TILES // 2, D // TILES, -1),
        "tile", 0, 0, axis_index_groups=core_groups,
    )
    chunks = list(near_total(high.reshape(1), parts))
    for place, moves in enumerate(far_rounds):
        chunks[1 + place] = lax.ppermute(chunks[1 + place], "head", far_moves(*moves))
    grad_w = tile_total(terms)
    grad_x = sum(chunk.astype(jnp.float32) for chunk in chunks).astype(jnp.bfloat16)
    return (grad_x, grad_w)


def solution(mesh):
    in_specs = (P("tile", None), P("head", None), P("tile", "head"), P("tile", None))
    out_specs = (P(("tile", "head"), None), P("tile", "head"))
    return jax.shard_map(local_step, mesh=mesh, in_specs=in_specs, out_specs=out_specs, check_vma=False)
```
